32 devices in a mesh: seq: 8 (over z, x), fsdp: 4 (over y, core).
Axes of the slice: x: 2, y: 2, z: 4, core: 2. Of those that a mesh axis runs over, the one named last changes fastest.
Arguments:
- layer_input: bfloat16 [4, 1024, 1024], P('fsdp', 'seq'), may hold values from -6 to 6
- doc_lengths: int32 [4, 5], replicated, may hold values from 1 to 512, 1024 in all within a row
- attn_gain: bfloat16 [1024], P(('seq', 'fsdp')), may hold values from 0.5 to 1.5
- qkv_weight: bfloat16 [1024, 3, 1024], P('seq', None, 'fsdp'), may hold values from -2 to 2
- out_weight: bfloat16 [1024, 1024], P('fsdp', 'seq'), may hold values from -0.5 to 0.5
- mlp_gain: bfloat16 [1024], P(('seq', 'fsdp')), may hold values from 0.5 to 1.5
- in_weight: bfloat16 [1024, 2, 2624], P('seq', None, 'fsdp'), may hold values from -0.1875 to 0.1875
- down_weight: bfloat16 [1024, 2624], P('seq', 'fsdp'), may hold values from -0.125 to 0.125
- out_grad: bfloat16 [4, 1024, 1024], P('fsdp', 'seq'), may hold values from -6 to 6
Outputs:
- layer_output: bfloat16 [4, 1024, 1024], P('fsdp', 'seq')
- input_grad: float32 [4, 1024, 1024], P('fsdp', 'seq')
- attn_gain_grad: float32 [1024], P(('seq', 'fsdp'))
- qkv_weight_grad: float32 [1024, 3, 1024], P('seq', None, 'fsdp')
- out_weight_grad: float32 [1024, 1024], P('fsdp', 'seq')
- mlp_gain_grad: float32 [1024], P(('seq', 'fsdp'))
- in_weight_grad: float32 [1024, 2, 2624], P('seq', None, 'fsdp')
- down_weight_grad: float32 [1024, 2624], P('seq', 'fsdp')
The draws below stay inside these ranges and needn't reach their ends.
Inputs may be any that keep to these rules, and one draw needn't show every extreme that they name: Each row of doc_lengths lists the lengths of the documents of one stream in order; they sum to 1024 and the longest is exactly 512.
All inputs are finite; a program needn't handle non-finite values.
Results may differ from the reference program's by a relative error of at most 0.02.
Values may be sent and summed in bfloat16 or wider, within the bound.
A program may use at most 128 MiB of HBM per device.

```python
import math
import jax
import jax.numpy as jnp
import numpy as np
from jax import lax

D = 1024
HEADS = 16
HEAD = 64
FF = 2624
WIN = 64
DOCS = 5
STREAM = 1024
N_FSDP = 4


def draw_qkv_weight(key, part):
    first = jax.random.fold_in(key, 11)
    second = jax.random.fold_in(key, 12)
    base = jax.random.normal(first, (D, 3 * D), jnp.float32) * D ** (-0.5)
    strength = jnp.exp(jax.random.uniform(second, (HEADS,), jnp.float32, math.log(0.5), math.log(2.0)))
    columns = jnp.repeat(strength, HEAD)[None, :]
    whole = jnp.concatenate([base[:, :2 * D] * jnp.concatenate([columns, columns], axis=1), base[:, 2 * D:]], axis=1)
    return jnp.clip(whole, -2.0, 2.0).reshape(D, 3, D).astype(jnp.bfloat16)


def with_spikes(drawn, rng, source, target, shards_of, factor):
    def block_of(axis_at):
        return (jnp.arange(drawn.shape[axis_at]) // (drawn.shape[axis_at] // shards_of)).reshape((-1,) + (1,) * (drawn.ndim - 1 - axis_at))

    near = jax.random.permutation(rng, shards_of)[block_of(target)]
    other_side = (block_of(target) + shards_of // 2) % shards_of
    return jnp.where((block_of(source) == near) | (block_of(source) == other_side), factor * drawn, drawn)


def level_of(key, extent, shards, smallest, high):
    level = 1.0
    for axis_at, parts in shards:
        heights = jax.random.uniform(jax.random.fold_in(jax.random.fold_in(key, 6), axis_at), (parts,), jnp.float32, smallest / len(shards), high / len(shards))
        level = level * jnp.repeat(jnp.exp(heights), extent[axis_at] // parts).reshape((-1,) + (1,) * (len(extent) - 1 - axis_at))
    return level


def length_profile(amount, total, most, skew):
    portions = [(1 << 20) // math.isqrt(grade ** skew) + 1 for grade in range(2, amount + 1)]
    spare, given = total - most - (amount - 1), [1] * (amount - 1)
    while spare > 0:
        movable = [i for i in range(amount - 1) if given[i] < most]
        pool, remaining = sum([portions[i] for i in movable]), spare
        for i in movable:
            extra = min(most - given[i], max(1, remaining * portions[i] // pool), spare)
            given[i] = given[i] + extra
            spare = spare - extra
    return np.array([most] + given)


def ragged_sizes(key, amount, total, bound, lean):
    if amount == 2:
        one = jax.random.randint(key, (), max(1, total - bound), min(bound, total - 1) + 1)
        return jnp.stack([one, total - one])
    tallies = jnp.asarray(length_profile(amount, total, bound, lean), jnp.int32)
    twos = (amount - 1) // 2
    source_of, sink = tallies[1:1 + 2 * twos:2], tallies[2:2 + 2 * twos:2]
    margin = jnp.minimum(source_of - 1, bound - sink)
    moved = jax.random.randint(jax.random.fold_in(key, 1), (twos,), 0, 1 << 20) % (margin + 1)
    tallies = tallies.at[1:1 + 2 * twos:2].set(source_of - moved).at[2:2 + 2 * twos:2].set(sink + moved)
    return tallies[jax.random.permutation(jax.random.fold_in(key, 2), amount)]


def normal_values(rng, extent, scale, most, cuts=(), kind=jnp.bfloat16):
    array = jax.random.normal(rng, extent, jnp.float32) * scale
    if len(cuts) > 0:
        array = level_of(rng, extent, cuts, -0.22, 0.18) * array
    return jnp.clip(array, min=-most, max=most).astype(kind)


def bell_draw_with(stream_key, shape, deviation, limit, cuts, heavy, kind=jnp.bfloat16):
    drawn = deviation * jax.random.normal(stream_key, shape, jnp.float32)
    if cuts:
        drawn = drawn * level_of(stream_key, shape, cuts, -0.22, 0.18)
    return jnp.clip(with_spikes(drawn, jax.random.fold_in(stream_key, 3), *heavy), -limit, limit).astype(kind)


def setup_inputs(seed: int = 0) -> dict:
    streams_of = jax.random.split(jax.random.key(seed), 10)
    return {
        "layer_input": normal_values(streams_of[0], (N_FSDP, STREAM, D), 1.0, 6.0, ((0, 4), (1, 8))),
        "doc_lengths": jax.vmap(lambda own: ragged_sizes(own, DOCS, STREAM, STREAM // 2, 2))(jax.random.split(streams_of[1], N_FSDP)).reshape((N_FSDP, DOCS)).astype(jnp.int32),
        "attn_gain": jnp.clip(1.0 + 0.1 * jax.random.normal(streams_of[2], (D,), jnp.float32), 0.5, 1.5).astype(jnp.bfloat16),
        "qkv_weight": draw_qkv_weight(jax.random.fold_in(streams_of[9], 71), 0),
        "out_weight": normal_values(streams_of[4], (D, D), (D // 8) ** -0.5, 0.5, ((0, 4), (1, 8))),
        "mlp_gain": jnp.clip(1.0 + 0.1 * jax.random.normal(streams_of[5], (D,), jnp.float32), 0.5, 1.5).astype(jnp.bfloat16),
        "in_weight": normal_values(streams_of[6], (D, 2, FF), D ** -0.5, 0.1875, ((0, 8), (2, 4))),
        "down_weight": normal_values(streams_of[7], (D, FF), FF ** -0.5, 0.125, ((0, 8), (1, 4))),
        "out_grad": bell_draw_with(streams_of[8], (N_FSDP, STREAM, D), 1.0, 6.0, ((0, 4), (1, 8)), (1, 2, 8, 2.0)),
    }


EPSILON = 1e-05

def norm_forward(values, gain):
    mean = lax.optimization_barrier(jnp.mean(values, axis=-1, keepdims=True))
    centred = values - mean
    inverse = lax.rsqrt(lax.optimization_barrier(jnp.mean(centred * centred, axis=-1, keepdims=True)) + EPSILON)
    scaled = centred * inverse
    return (scaled, inverse, (scaled * gain.astype(jnp.float32)).astype(jnp.bfloat16))

def norm_backward(grad, scaled, inverse, gain):
    weighted = grad * gain.astype(jnp.float32)
    back = inverse * (weighted - lax.optimization_barrier(jnp.mean(weighted, axis=-1, keepdims=True)) - scaled * lax.optimization_barrier(jnp.mean(weighted * scaled, axis=-1, keepdims=True)))
    return (back, lax.optimization_barrier(jnp.sum(grad * scaled, axis=0)))

def gelu_parts(inner):
    cdf = 0.5 * (1.0 + jax.scipy.special.erf(inner * 0.7071067811865476))
    density = jnp.exp(-0.5 * inner * inner) * 0.3989422804014327
    return (inner * cdf, cdf + inner * density)

def rope_tables(positions, head_size):
    half = head_size // 2
    inv_freq = 10000.0 ** (-(2.0 / head_size) * jnp.arange(half, dtype=jnp.float32))
    angle = positions.astype(jnp.float32)[:, None] * inv_freq[None, :]
    return (jnp.cos(angle)[:, None, :], jnp.sin(angle)[:, None, :])

def rotate(field, cosine, sine):
    half = field.shape[-1] // 2
    first, second = (field[..., :half], field[..., half:])
    return jnp.concatenate([first * cosine - second * sine, second * cosine + first * sine], axis=-1)

def unrotate(grad, cosine, sine):
    half = grad.shape[-1] // 2
    first, second = (grad[..., :half], grad[..., half:])
    return jnp.concatenate([first * cosine + second * sine, second * cosine - first * sine], axis=-1)

def doc_ids(lengths_row, positions):
    starts = jnp.cumsum(lengths_row, dtype=jnp.int32) - lengths_row
    total = jnp.sum(lengths_row, dtype=jnp.int32)
    found = lax.optimization_barrier(jnp.sum((positions[:, None] >= starts[None, :]).astype(jnp.int32), axis=1, dtype=jnp.int32)) - 1
    valid = (positions >= 0) & (positions < total)
    return jnp.where(valid, found, -1).astype(jnp.int32)

def window_mask(ids_query, ids_key, reach):
    block = ids_query.shape[0]
    offset = jnp.arange(block, dtype=jnp.int32)[:, None] + reach - jnp.arange(block + 2 * reach, dtype=jnp.int32)[None, :]
    return (jnp.abs(offset) <= reach) & (ids_query[:, None] == ids_key[None, :])

def attend_forward(query, keys, values, allowed):
    scale = query.shape[-1] ** (-0.5)
    scores = jnp.einsum('nhe,mhe->hnm', query.astype(jnp.float32), keys.astype(jnp.float32)) * scale
    masked = jnp.where(allowed[None], scores, -1e+30)
    top = lax.optimization_barrier(jnp.max(masked, axis=-1, keepdims=True))
    expd = jnp.exp(masked - top)
    total = lax.optimization_barrier(jnp.sum(expd, axis=-1, keepdims=True))
    log_total = (top + jnp.log(total))[..., 0]
    probs = (expd / total).astype(jnp.bfloat16)
    out = jnp.einsum('hnm,mhe->nhe', probs.astype(jnp.float32), values.astype(jnp.float32))
    return (out.astype(jnp.bfloat16), log_total)

def attend_backward(query, keys, values, allowed, log_total, attended, grad_out):
    scale = query.shape[-1] ** (-0.5)
    scores = jnp.einsum('nhe,mhe->hnm', query.astype(jnp.float32), keys.astype(jnp.float32)) * scale
    masked = jnp.where(allowed[None], scores, -1e+30)
    again = jnp.exp(masked - log_total[..., None])
    again_b = again.astype(jnp.bfloat16)
    grad_f = grad_out.astype(jnp.float32)
    grad_values = jnp.einsum('hnm,nhe->mhe', again_b.astype(jnp.float32), grad_f)
    grad_probs = jnp.einsum('nhe,mhe->hnm', grad_f, values.astype(jnp.float32))
    delta = lax.optimization_barrier(jnp.sum(grad_f * attended.astype(jnp.float32), axis=-1)).T
    grad_scores = (again * (grad_probs - delta[..., None]) * scale).astype(jnp.bfloat16).astype(jnp.float32)
    grad_query = jnp.einsum('hnm,mhe->nhe', grad_scores, keys.astype(jnp.float32))
    grad_keys = jnp.einsum('hnm,nhe->mhe', grad_scores, query.astype(jnp.float32))
    return (grad_query, grad_keys, grad_values)

def attention_forward(query, ext_keys, ext_values, ids_query, ids_key, block, reach):
    rows, heads = (query.shape[0], query.shape[1])
    count = rows // block

    def step(carry, index):
        start = index * block
        q_block = lax.dynamic_slice_in_dim(query, start, block, 0)
        k_block = lax.dynamic_slice_in_dim(ext_keys, start, block + 2 * reach, 0)
        v_block = lax.dynamic_slice_in_dim(ext_values, start, block + 2 * reach, 0)
        allowed = window_mask(lax.dynamic_slice_in_dim(ids_query, start, block, 0), lax.dynamic_slice_in_dim(ids_key, start, block + 2 * reach, 0), reach)
        return (carry, attend_forward(q_block, k_block, v_block, allowed))
    _, (outs, totals) = lax.scan(step, jnp.zeros((), jnp.float32), jnp.arange(count, dtype=jnp.int32))
    return (outs.reshape(rows, heads, -1), totals.transpose(1, 0, 2).reshape(heads, rows))

def attention_backward(query, ext_keys, ext_values, ids_query, ids_key, log_total, attended, grad_out, block, reach):
    rows = query.shape[0]
    count = rows // block
    zero = jnp.zeros(ext_keys.shape, jnp.float32)

    def step(carry, index):
        keys_acc, values_acc = carry
        start = index * block
        span = block + 2 * reach
        q_block = lax.dynamic_slice_in_dim(query, start, block, 0)
        k_block = lax.dynamic_slice_in_dim(ext_keys, start, span, 0)
        v_block = lax.dynamic_slice_in_dim(ext_values, start, span, 0)
        allowed = window_mask(lax.dynamic_slice_in_dim(ids_query, start, block, 0), lax.dynamic_slice_in_dim(ids_key, start, span, 0), reach)
        lse_block = lax.dynamic_slice_in_dim(log_total, start, block, 1)
        a_block = lax.dynamic_slice_in_dim(attended, start, block, 0)
        g_block = lax.dynamic_slice_in_dim(grad_out, start, block, 0)
        grad_query, grad_keys, grad_values = attend_backward(q_block, k_block, v_block, allowed, lse_block, a_block, g_block)
        keys_acc = lax.dynamic_update_slice_in_dim(keys_acc, lax.dynamic_slice_in_dim(keys_acc, start, span, 0) + grad_keys, start, 0)
        values_acc = lax.dynamic_update_slice_in_dim(values_acc, lax.dynamic_slice_in_dim(values_acc, start, span, 0) + grad_values, start, 0)
        return ((keys_acc, values_acc), grad_query)
    (keys_acc, values_acc), grads = lax.scan(step, (zero, zero), jnp.arange(count, dtype=jnp.int32))
    return (grads.reshape(query.shape), keys_acc, values_acc)

def stream_layer(tokens, lengths_row, attn_gain, qkv_weight, out_weight, mlp_gain, in_weight, down_weight, grad_rows):
    rows = tokens.shape[0]
    width = tokens.shape[1]
    heads = attn_gain.shape[0] // HEAD
    hidden_units = down_weight.shape[1]
    reach = WIN
    block = min(rows, 512)
    positions = jnp.arange(rows, dtype=jnp.int32)
    outer = jnp.arange(rows + 2 * reach, dtype=jnp.int32) - reach
    ids_query = doc_ids(lengths_row, positions)
    ids_key = doc_ids(lengths_row, outer)
    cosine, sine = rope_tables(positions, HEAD)
    resid_in = tokens.astype(jnp.float32)
    scaled_one, inverse_one, normed_one = norm_forward(resid_in, attn_gain)
    projected = jnp.dot(normed_one, qkv_weight, preferred_element_type=jnp.float32)
    split = projected.reshape(rows, 3, heads, HEAD)
    query = rotate(split[:, 0], cosine, sine).astype(jnp.bfloat16)
    keys = rotate(split[:, 1], cosine, sine).astype(jnp.bfloat16)
    values = split[:, 2].astype(jnp.bfloat16)
    padding = ((reach, reach), (0, 0), (0, 0))
    ext_keys = jnp.pad(keys, padding)
    ext_values = jnp.pad(values, padding)
    attended, log_total = attention_forward(query, ext_keys, ext_values, ids_query, ids_key, block, reach)
    attended_flat = attended.reshape(rows, width)
    middle = resid_in + jnp.dot(attended_flat, out_weight, preferred_element_type=jnp.float32)
    scaled_two, inverse_two, normed_two = norm_forward(middle, mlp_gain)
    hidden = jnp.dot(normed_two, in_weight, preferred_element_type=jnp.float32)
    inner, gate = (hidden[:, :hidden_units], hidden[:, hidden_units:])
    activated, slope = gelu_parts(inner)
    mixed = (activated * gate).astype(jnp.bfloat16)
    projected_down = lax.dot_general(mixed, down_weight, (((1,), (1,)), ((), ())), preferred_element_type=jnp.float32)
    output = (middle + projected_down).astype(jnp.bfloat16)
    grad_down = lax.dot_general(grad_rows, mixed, (((0,), (0,)), ((), ())), preferred_element_type=jnp.float32)
    grad_mixed = jnp.dot(grad_rows, down_weight, preferred_element_type=jnp.float32)
    grad_hidden = jnp.concatenate([grad_mixed * gate * slope, grad_mixed * activated], axis=1).astype(jnp.bfloat16)
    grad_in = lax.dot_general(normed_two, grad_hidden, (((0,), (0,)), ((), ())), preferred_element_type=jnp.float32)
    grad_normed_two = lax.dot_general(grad_hidden, in_weight, (((1,), (1,)), ((), ())), preferred_element_type=jnp.float32)
    back_two, grad_gain_two = norm_backward(grad_normed_two, scaled_two, inverse_two, mlp_gain)
    grad_middle = grad_rows.astype(jnp.float32) + back_two
    grad_middle_b = grad_middle.astype(jnp.bfloat16)
    grad_out_weight = lax.dot_general(attended_flat, grad_middle_b, (((0,), (0,)), ((), ())), preferred_element_type=jnp.float32)
    grad_attended = lax.dot_general(grad_middle_b, out_weight, (((1,), (1,)), ((), ())), preferred_element_type=jnp.float32).astype(jnp.bfloat16)
    grad_query, keys_acc, values_acc = attention_backward(query, ext_keys, ext_values, ids_query, ids_key, log_total, attended, grad_attended.reshape(rows, heads, HEAD), block, reach)
    grad_keys = unrotate(keys_acc[reach:reach + rows], cosine, sine)
    grad_values = values_acc[reach:reach + rows]
    grad_query = unrotate(grad_query, cosine, sine)
    grad_projected = jnp.concatenate([grad_query.reshape(rows, width), grad_keys.reshape(rows, width), grad_values.reshape(rows, width)], axis=1).astype(jnp.bfloat16)
    grad_qkv = lax.dot_general(normed_one, grad_projected, (((0,), (0,)), ((), ())), preferred_element_type=jnp.float32)
    grad_normed_one = lax.dot_general(grad_projected, qkv_weight, (((1,), (1,)), ((), ())), preferred_element_type=jnp.float32)
    back_one, grad_gain_one = norm_backward(grad_normed_one, scaled_one, inverse_one, attn_gain)
    input_grad = grad_middle + back_one
    return (output, input_grad, (grad_gain_one, grad_qkv, grad_out_weight, grad_gain_two, grad_in, grad_down))

def reference(layer_input, doc_lengths, attn_gain, qkv_weight, out_weight, mlp_gain, in_weight, down_weight, out_grad):
    qkv_flat = qkv_weight.reshape(D, 3 * D)
    in_flat = in_weight.reshape(D, 2 * FF)
    outputs = []
    inputs_grads = []
    sums = None
    for stream in range(N_FSDP):
        output, input_grad, grads = stream_layer(layer_input[stream], doc_lengths[stream], attn_gain, qkv_flat, out_weight, mlp_gain, in_flat, down_weight, out_grad[stream])
        outputs.append(output)
        inputs_grads.append(input_grad)
        if sums is None:
            sums = grads
        else:
            sums = tuple((left + right for left, right in zip(sums, grads)))
    return (jnp.stack(outputs), jnp.stack(inputs_grads), sums[0], sums[1].reshape(D, 3, D), sums[2], sums[3], sums[4].reshape(D, 2, FF), sums[5])
```

```python
import functools

import jax
import jax.numpy as jnp
from jax import lax
from jax.experimental import pallas as pl
from jax.experimental.pallas import tpu as pltpu
from jax.sharding import PartitionSpec as P

HEAD = 64
WIN = 64


EPSILON = 1e-05


class Place:
    def __init__(self, axis):
        self.axis = axis
        self.n = lax.axis_size(axis)
        self.length = self.n // 2
        me = lax.axis_index(axis)
        self.me = me
        self.at = me // 2
        self.side = me % 2

    def partner(self):
        return {self.axis: self.at * 2 + (1 - self.side)}

    def right(self):
        return {self.axis: self.me + 2}

    def left(self):
        return {self.axis: self.me - 2}

    def has_right(self):
        return self.at < self.length - 1

    def has_left(self):
        return self.at > 0

    def greet(self, barrier):
        mesh = pl.DeviceIdType.MESH
        pl.semaphore_signal(barrier, inc=1, device_id=self.partner(), device_id_type=mesh)

        @pl.when(self.has_left())
        def _():
            pl.semaphore_signal(barrier, inc=1, device_id=self.left(), device_id_type=mesh)

        @pl.when(self.has_right())
        def _():
            pl.semaphore_signal(barrier, inc=1, device_id=self.right(), device_id_type=mesh)

    def peers(self):
        one, none = jnp.int32(1), jnp.int32(0)
        return 1 + jnp.where(self.has_left(), one, none) + jnp.where(self.has_right(), one, none)


def remote(src, dst, send, recv, device):
    return pltpu.make_async_remote_copy(
        src_ref=src,
        dst_ref=dst,
        send_sem=send,
        recv_sem=recv,
        device_id=device,
        device_id_type=pl.DeviceIdType.MESH,
    )


class Gather:
    scratch = staticmethod(
        lambda n: [
            pltpu.SemaphoreType.DMA((3, n)),
            pltpu.SemaphoreType.DMA((n,)),
            pltpu.SemaphoreType.DMA,
        ]
    )

    def __init__(self, place, src, dst, sems):
        self.place, self.src, self.dst = place, src, dst
        self.send, self.recv, self.local = sems

    def copy(self, way, block, device, own=False):
        src = self.src if own else self.dst.at[block]
        return remote(src, self.dst.at[block], self.send.at[way, block], self.recv.at[block], device)

    def onward(self, block, own, act):
        place = self.place
        act(self.copy(0, block, place.partner(), own))

    def start(self):
        place = self.place
        pltpu.make_async_copy(self.src, self.dst.at[place.me], self.local).start()
        self.ahead(place.me, True, lambda c: c.start())
        self.behind(place.me, True, lambda c: c.start())
        self.onward(place.me, True, lambda c: c.start())

    def ahead(self, block, own, act):
        place = self.place

        @pl.when(place.has_right())
        def _():
            act(self.copy(1, block, place.right(), own))

    def behind(self, block, own, act):
        place = self.place

        @pl.when(place.has_left())
        def _():
            act(self.copy(2, block, place.left(), own))

    def step(self, d):
        place = self.place

        @pl.when(place.at - d >= 0)
        def _():
            block = place.me - 2 * d
            self.copy(1, block, place.partner()).wait_recv()
            self.ahead(block, False, lambda c: c.start())
            self.onward(block, False, lambda c: c.start())

        @pl.when(place.at + d < place.length)
        def _():
            block = place.me + 2 * d
            self.copy(2, block, place.partner()).wait_recv()
            self.behind(block, False, lambda c: c.start())
            self.onward(block, False, lambda c: c.start())

    def finish(self):
        place = self.place
        pltpu.make_async_copy(self.src, self.dst.at[place.me], self.local).wait()

        def arrived(i, carry):
            self.copy(0, 2 * i + 1 - place.side, place.partner()).wait_recv()
            self.onward(2 * i + place.side, False, lambda c: c.wait_send())

            @pl.when(i <= place.at)
            def _():
                self.ahead(2 * i + place.side, False, lambda c: c.wait_send())

            @pl.when(i >= place.at)
            def _():
                self.behind(2 * i + place.side, False, lambda c: c.wait_send())

            return carry

        lax.fori_loop(0, place.length, arrived, 0)


class Reduce:
    @staticmethod
    def scratch(n, block, dtype):
        length = n // 2
        return [
            pltpu.VMEM((length,) + block, dtype),
            pltpu.VMEM((length,) + block, dtype),
            pltpu.VMEM((length + 1,) + block, dtype),
            pltpu.SemaphoreType.DMA((2, length)),
            pltpu.SemaphoreType.DMA((length,)),
            pltpu.SemaphoreType.DMA((length + 1,)),
        ]

    def __init__(self, place, src, dst, scratch):
        self.place, self.src, self.dst = place, src, dst
        self.stage, self.paired, self.lined, self.send, self.pair_recv, self.line_recv = scratch

    def across(self, i):
        place = self.place
        return remote(
            self.src.at[2 * i + 1 - place.side],
            self.paired.at[i],
            self.send.at[0, i],
            self.pair_recv.at[i],
            place.partner(),
        )

    def along(self, i, slot, device):
        return remote(
            self.stage.at[i], self.lined.at[slot], self.send.at[1, i], self.line_recv.at[slot], device
        )

    def start(self):
        place = self.place

        def each(k, carry):
            d = place.length - 1 - k

            @pl.when(place.at + d < place.length)
            def _():
                self.across(place.at + d).start()

            @pl.when(jnp.logical_and(d > 0, place.at - d >= 0))
            def _():
                self.across(place.at - d).start()

            return carry

        lax.fori_loop(0, place.length, each, 0)

    def add(self, out, refs):
        rows = out.shape[0]
        tile = 16 if rows % 16 == 0 else 8

        def each(i, carry):
            at = pl.ds(pl.multiple_of(i * tile, tile), tile)
            total = refs[0][at, :].astype(jnp.float32)
            for ref in refs[1:]:
                total = total + ref[at, :].astype(jnp.float32)
            out[at, :] = total.astype(out.dtype)
            return carry

        lax.fori_loop(0, rows // tile, each, 0)

    def own(self, i):
        self.across(i).wait_recv()
        return [self.src.at[2 * i + self.place.side], self.paired.at[i]]

    def step(self, d):
        place = self.place

        @pl.when(place.at + d < place.length)
        def _():
            i = place.at + d
            refs = self.own(i)

            @pl.when(place.has_left())
            def _():
                self.along(i, i, place.partner()).wait_recv()
                self.add(self.stage.at[i], refs + [self.lined.at[i]])

            @pl.when(jnp.logical_not(place.has_left()))
            def _():
                self.add(self.stage.at[i], refs)

            self.along(i, i, place.right()).start()

        @pl.when(place.at - d >= 0)
        def _():
            i = place.at - d
            refs = self.own(i)

            @pl.when(place.has_right())
            def _():
                self.along(i, i, place.partner()).wait_recv()
                self.add(self.stage.at[i], refs + [self.lined.at[i]])

            @pl.when(jnp.logical_not(place.has_right()))
            def _():
                self.add(self.stage.at[i], refs)

            slot = jnp.where(d == 1, place.length, i)
            self.along(i, slot, place.left()).start()

    def last(self):
        place = self.place
        i, extra = place.at, place.length
        refs = self.own(i)

        @pl.when(place.has_left())
        def _():
            self.along(i, i, place.partner()).wait_recv()

        @pl.when(place.has_right())
        def _():
            self.along(i, extra, place.partner()).wait_recv()

        both = jnp.logical_and(place.has_left(), place.has_right())

        @pl.when(both)
        def _():
            self.add(self.dst, refs + [self.lined.at[i], self.lined.at[extra]])

        @pl.when(jnp.logical_and(place.has_left(), jnp.logical_not(both)))
        def _():
            self.add(self.dst, refs + [self.lined.at[i]])

        @pl.when(jnp.logical_and(place.has_right(), jnp.logical_not(both)))
        def _():
            self.add(self.dst, refs + [self.lined.at[extra]])

    def finish(self):
        place = self.place

        def each(i, carry):
            self.across(i).wait_send()

            @pl.when(i != place.at)
            def _():
                self.along(i, i, place.partner()).wait_send()

            return carry

        lax.fori_loop(0, place.length, each, 0)


def greet_all(places):
    barrier = pltpu.get_barrier_semaphore()
    for place in places:
        place.greet(barrier)
    pl.semaphore_wait(barrier, sum(place.peers() for place in places))


def steps(jobs, down):
    length = jobs[0].place.length

    def each(k, carry):
        d = length - 1 - k if down else k + 1
        for job in jobs:
            job.step(d)
        return carry

    lax.fori_loop(0, length - 1, each, 0)


def take(items, count):
    return items[:count], items[count:]


def comm_kernel(plan, *refs):
    seq, fsdp = Place("seq"), Place("fsdp")
    places = {"seq": seq, "fsdp": fsdp}
    ins, rest = take(list(refs), len(plan))
    outs, scratch = take(rest, len(plan))
    jobs = []
    for (kind, axis), src, dst in zip(plan, ins, outs):
        place = places[axis]
        if kind == "gather":
            own, scratch = take(scratch, 3)
            jobs.append((kind, axis, Gather(place, src, dst, own), None))
        elif kind == "reduce":
            own, scratch = take(scratch, 6)
            jobs.append((kind, axis, Reduce(place, src, dst, own), None))
        elif kind == "sum":
            own, scratch = take(scratch, 6)
            mid, scratch = take(scratch, 1)
            sems, scratch = take(scratch, 3)
            jobs.append((kind, axis, Reduce(place, src, mid[0], own), Gather(place, mid[0], dst, sems)))
        elif kind == "gather2":
            own, scratch = take(scratch, 3)
            mid, scratch = take(scratch, 1)
            sems, scratch = take(scratch, 3)
            jobs.append((kind, axis, Gather(seq, src, mid[0], own), Gather(fsdp, mid[0], dst, sems)))
        elif kind == "reduce2":
            own, scratch = take(scratch, 6)
            mid, scratch = take(scratch, 1)
            sems, scratch = take(scratch, 3)
            jobs.append((kind, axis, Reduce(seq, src, mid[0], own), Gather(fsdp, mid[0], dst, sems)))
    greet_all((seq, fsdp))
    ga = [j for k, a, j, _ in jobs if a == "seq" and isinstance(j, Gather)]
    gb = [j for k, a, j, _ in jobs if a == "fsdp" and isinstance(j, Gather)]
    ra = [j for k, a, j, _ in jobs if a == "seq" and isinstance(j, Reduce)]
    rb = [j for k, a, j, _ in jobs if a == "fsdp" and isinstance(j, Reduce)]
    second = [j for k, a, _, j in jobs if k == "sum"]
    late = [j for k, a, _, j in jobs if k in ("gather2", "reduce2")]
    for job in rb + ra + gb + ga:
        job.start()
    if rb:
        steps(rb, True)
    if ga:
        steps(ga, False)
    if gb:
        steps(gb, False)
    for job in rb:
        job.last()
    for job in second:
        job.start()
    if ra:
        steps(ra, True)
    for job in ra:
        job.last()
    if second:
        steps(second, False)
    for job in ga:
        job.finish()
    for job in late:
        job.start()
    if late:
        steps(late, False)
    for job in gb + rb + ra + second + late:
        job.finish()


def communicate(number, jobs):
    sizes = {axis: lax.axis_size(axis) for axis in ("seq", "fsdp")}
    shapes, scratch = [], []
    for kind, axis, array, dtype in jobs:
        n = sizes[axis]
        if kind == "gather":
            shapes.append((n,) + array.shape)
            scratch += Gather.scratch(n)
        elif kind == "gather2":
            shapes.append((sizes["fsdp"], n) + array.shape)
            scratch += Gather.scratch(n)
            scratch += [pltpu.VMEM((n,) + array.shape, array.dtype)] + Gather.scratch(sizes["fsdp"])
        else:
            block = array.shape[1:]
            scratch += Reduce.scratch(n, block, array.dtype)
            if kind == "reduce":
                shapes.append(block)
            elif kind == "sum":
                shapes.append(array.shape)
                scratch += [pltpu.VMEM(block, dtype)] + Gather.scratch(n)
            else:
                shapes.append((sizes["fsdp"],) + block)
                scratch += [pltpu.VMEM(block, dtype)] + Gather.scratch(sizes["fsdp"])
    vmem = pl.BlockSpec(memory_space=pltpu.VMEM)
    return pl.pallas_call(
        functools.partial(comm_kernel, tuple((kind, axis) for kind, axis, _, _ in jobs)),
        out_shape=[jax.ShapeDtypeStruct(s, j[3]) for s, j in zip(shapes, jobs)],
        in_specs=[vmem] * len(jobs),
        out_specs=[vmem] * len(jobs),
        scratch_shapes=scratch,
        compiler_params=pltpu.CompilerParams(
            collective_id=number, has_side_effects=True, vmem_limit_bytes=60 * 1024 * 1024
        ),
    )(*[array for _, _, array, _ in jobs])


def with_halo(value, sides, width):
    for axis, dim in sides:
        devices, length = (lax.axis_size(axis), value.shape[dim])
        up = [(i, (i + 1) % devices) for i in range(devices - 1)]
        down = [(j, i) for i, j in up]
        last = lax.slice_in_dim(value, length - width, length, axis=dim)
        first = lax.slice_in_dim(value, 0, width, axis=dim)
        before = lax.ppermute(last, axis, up)
        after = lax.ppermute(first, axis, down)
        value = jnp.concatenate([before, value, after], axis=dim)
    return value


def norm_forward(values, gain):
    mean = jnp.mean(values, axis=-1, keepdims=True)
    centred = values - mean
    inverse = lax.rsqrt(jnp.mean(centred * centred, axis=-1, keepdims=True) + EPSILON)
    scaled = centred * inverse
    return (scaled, inverse, (scaled * gain.astype(jnp.float32)).astype(jnp.bfloat16))


def norm_backward(grad, scaled, inverse, gain):
    weighted = grad * gain.astype(jnp.float32)
    back = inverse * (
        weighted
        - jnp.mean(weighted, axis=-1, keepdims=True)
        - scaled * jnp.mean(weighted * scaled, axis=-1, keepdims=True)
    )
    return back


def gelu_parts(inner):
    cdf = 0.5 * (1.0 + jax.scipy.special.erf(inner * 0.7071067811865476))
    density = jnp.exp(-0.5 * inner * inner) * 0.3989422804014327
    return (inner * cdf, cdf + inner * density)


def rope_tables(positions, head_size):
    half = head_size // 2
    inv_freq = 10000.0 ** (-(2.0 / head_size) * jnp.arange(half, dtype=jnp.float32))
    angle = positions.astype(jnp.float32)[:, None] * inv_freq[None, :]
    return (jnp.cos(angle)[:, None, :], jnp.sin(angle)[:, None, :])


def rotate(field, cosine, sine):
    half = field.shape[-1] // 2
    first, second = (field[..., :half], field[..., half:])
    return jnp.concatenate(
        [first * cosine - second * sine, second * cosine + first * sine], axis=-1
    )


def unrotate(grad, cosine, sine):
    half = grad.shape[-1] // 2
    first, second = (grad[..., :half], grad[..., half:])
    return jnp.concatenate(
        [first * cosine + second * sine, second * cosine - first * sine], axis=-1
    )


def doc_ids(lengths_row, positions):
    starts = jnp.cumsum(lengths_row, dtype=jnp.int32) - lengths_row
    total = jnp.sum(lengths_row, dtype=jnp.int32)
    found = (
        jnp.sum((positions[:, None] >= starts[None, :]).astype(jnp.int32), axis=1, dtype=jnp.int32)
        - 1
    )
    valid = (positions >= 0) & (positions < total)
    return jnp.where(valid, found, -1)


def window_mask(ids_query, ids_key, reach):
    block = ids_query.shape[0]
    offset = (
        jnp.arange(block, dtype=jnp.int32)[:, None]
        + reach
        - jnp.arange(block + 2 * reach, dtype=jnp.int32)[None, :]
    )
    return (jnp.abs(offset) <= reach) & (ids_query[:, None] == ids_key[None, :])


def attend_forward(query, keys, values, allowed):
    scale = query.shape[-1] ** (-0.5)
    scores = jnp.einsum("nhe,mhe->hnm", query, keys, preferred_element_type=jnp.float32) * scale
    masked = jnp.where(allowed[None], scores, -1e30)
    top = jnp.max(masked, axis=-1, keepdims=True)
    expd = jnp.exp(masked - top)
    total = jnp.sum(expd, axis=-1, keepdims=True)
    log_total = (top + jnp.log(total))[..., 0]
    probs = (expd / total).astype(jnp.bfloat16)
    out = jnp.einsum("hnm,mhe->nhe", probs, values, preferred_element_type=jnp.float32)
    return (out.astype(jnp.bfloat16), log_total)


def attend_backward(query, keys, values, allowed, log_total, attended, grad_out):
    scale = query.shape[-1] ** (-0.5)
    scores = jnp.einsum("nhe,mhe->hnm", query, keys, preferred_element_type=jnp.float32) * scale
    masked = jnp.where(allowed[None], scores, -1e30)
    again = jnp.exp(masked - log_total[..., None])
    again_b = again.astype(jnp.bfloat16)
    grad_values = jnp.einsum("hnm,nhe->mhe", again_b, grad_out, preferred_element_type=jnp.float32)
    grad_probs = jnp.einsum("nhe,mhe->hnm", grad_out, values, preferred_element_type=jnp.float32)
    delta = jnp.sum(grad_out.astype(jnp.float32) * attended.astype(jnp.float32), axis=-1).T
    grad_scores = (again * (grad_probs - delta[..., None]) * scale).astype(jnp.bfloat16)
    grad_query = jnp.einsum("hnm,mhe->nhe", grad_scores, keys, preferred_element_type=jnp.float32)
    grad_keys = jnp.einsum("hnm,nhe->mhe", grad_scores, query, preferred_element_type=jnp.float32)
    return (grad_query, grad_keys, grad_values)


def attention_forward(query, ext_keys, ext_values, ids_query, ids_key, block, reach):
    rows, heads = (query.shape[0], query.shape[1])
    count = rows // block

    def step(carry, index):
        allowed = window_mask(ids_query, ids_key, reach)
        return (carry, attend_forward(query, ext_keys, ext_values, allowed))

    _, (outs, totals) = lax.scan(
        step, jnp.zeros((), jnp.float32), jnp.arange(count, dtype=jnp.int32)
    )
    return (outs.reshape(rows, heads, -1), totals.transpose(1, 0, 2).reshape(heads, rows))


def attention_backward(
    query, ext_keys, ext_values, ids_query, ids_key, log_total, attended, grad_out, block, reach
):
    rows = query.shape[0]
    count = rows // block
    zero = jnp.zeros(ext_keys.shape, jnp.float32)

    def step(carry, index):
        keys_acc, values_acc = carry
        allowed = window_mask(ids_query, ids_key, reach)
        grad_query, grad_keys, grad_values = attend_backward(
            query, ext_keys, ext_values, allowed, log_total, attended, grad_out
        )
        keys_acc = keys_acc + grad_keys
        values_acc = values_acc + grad_values
        return ((keys_acc, values_acc), grad_query)

    (keys_acc, values_acc), grads = lax.scan(step, (zero, zero), jnp.arange(count, dtype=jnp.int32))
    return (grads.reshape(query.shape), keys_acc, values_acc)


def per_device(
    layer_input,
    doc_lengths,
    attn_gain,
    qkv_weight,
    out_weight,
    mlp_gain,
    in_weight,
    down_weight,
    out_grad,
):
    tokens = layer_input[0]
    grad_rows = out_grad[0]
    rows, width = tokens.shape
    streams = doc_lengths.shape[0]
    quarter = qkv_weight.shape[2]
    heads_here = quarter // HEAD
    share = down_weight.shape[1]
    reach = WIN
    block = min(rows, 512)
    n_seq, n_fsdp = lax.axis_size("seq"), lax.axis_size("fsdp")
    stream = lax.axis_index("fsdp")
    part = width // n_seq
    piece = attn_gain.shape[0]
    b16, f32 = jnp.bfloat16, jnp.float32
    first = lax.axis_index("seq") * rows
    positions = first + jnp.arange(rows, dtype=jnp.int32)
    outer = first - reach + jnp.arange(rows + 2 * reach, dtype=jnp.int32)
    ids_query = jax.vmap(doc_ids, in_axes=(0, None))(doc_lengths, positions)
    ids_key = jax.vmap(doc_ids, in_axes=(0, None))(doc_lengths, outer)
    cosine, sine = rope_tables(positions, HEAD)
    gains = jnp.pad(jnp.stack([attn_gain, mlp_gain]), ((0, 14), (0, 128 - piece)))
    gains_all, tokens_all, grad_all, qkv_all, out_all, in_all, down_all = communicate(
        1,
        [
            ("gather2", "seq", gains, b16),
            ("gather", "fsdp", tokens, b16),
            ("gather", "fsdp", grad_rows, b16),
            ("gather", "seq", qkv_weight.reshape(part, 3 * quarter), b16),
            ("gather", "seq", out_weight, b16),
            ("gather", "seq", in_weight.reshape(part, 2 * share), b16),
            ("gather", "seq", down_weight, b16),
        ],
    )
    gain_one = gains_all[:, :, 0, :piece].transpose(1, 0, 2).reshape(width)
    gain_two = gains_all[:, :, 1, :piece].transpose(1, 0, 2).reshape(width)
    qkv_flat = qkv_all.reshape(width, 3 * quarter)
    in_flat = in_all.reshape(width, 2 * share)
    down_full = down_all.reshape(width, share)
    out_rows = out_all.transpose(1, 0, 2).reshape(quarter, width)
    grad_flat = grad_all.reshape(streams * rows, width)
    resid_in = tokens_all.reshape(streams * rows, width).astype(f32)
    scaled_one, inverse_one, group_one = norm_forward(resid_in, gain_one)
    projected = jnp.dot(group_one, qkv_flat, preferred_element_type=f32)
    split = projected.reshape(streams, rows, 3, heads_here, HEAD)
    query = rotate(split[:, :, 0], cosine, sine).astype(b16)
    keys = rotate(split[:, :, 1], cosine, sine).astype(b16)
    values = split[:, :, 2].astype(b16)
    packed = jnp.concatenate(
        [keys.reshape(streams, rows, quarter), values.reshape(streams, rows, quarter)], axis=2
    )
    extended = with_halo(packed, (("seq", 1),), WIN)
    ext_keys = extended[:, :, :quarter].reshape(streams, -1, heads_here, HEAD)
    ext_values = extended[:, :, quarter:].reshape(streams, -1, heads_here, HEAD)

    def forward_stream(stream_query, stream_keys, stream_values, stream_ids, stream_key_ids):
        return attention_forward(
            stream_query, stream_keys, stream_values, stream_ids, stream_key_ids, block, reach
        )

    attended, log_total = jax.vmap(forward_stream)(query, ext_keys, ext_values, ids_query, ids_key)
    attended_flat = attended.reshape(streams * rows, quarter)
    partial_attn = jnp.dot(attended_flat, out_rows, preferred_element_type=f32)
    (attn_sum,) = communicate(
        2, [("sum", "fsdp", partial_attn.astype(b16).reshape(streams, rows, width), b16)]
    )
    middle = resid_in + attn_sum.reshape(streams * rows, width).astype(f32)
    scaled_two, inverse_two, normed_flat = norm_forward(middle, gain_two)
    hidden = jnp.dot(normed_flat, in_flat, preferred_element_type=f32)
    inner, gate = (hidden[:, :share], hidden[:, share:])
    activated, slope = gelu_parts(inner)
    mixed = (activated * gate).astype(b16)
    partial_down = lax.dot_general(
        mixed, down_full, (((1,), (1,)), ((), ())), preferred_element_type=f32
    )
    grad_down = lax.dot_general(
        grad_flat, mixed, (((0,), (0,)), ((), ())), preferred_element_type=f32
    )
    grad_mixed = jnp.dot(grad_flat, down_full, preferred_element_type=f32)
    grad_hidden = jnp.concatenate(
        [grad_mixed * gate * slope, grad_mixed * activated], axis=1
    ).astype(b16)
    grad_in = lax.dot_general(
        normed_flat, grad_hidden, (((0,), (0,)), ((), ())), preferred_element_type=f32
    )
    partial_back = lax.dot_general(
        grad_hidden, in_flat, (((1,), (1,)), ((), ())), preferred_element_type=f32
    )
    grad_gain_two = jnp.sum(partial_back * scaled_two, axis=0)
    back_sum, down_sum, summed_in, summed_down = communicate(
        3,
        [
            ("sum", "fsdp", partial_back.astype(b16).reshape(streams, rows, width), b16),
            ("reduce", "fsdp", partial_down.astype(b16).reshape(streams, rows, width), f32),
            ("reduce", "seq", grad_in.astype(b16).reshape(n_seq, part, 2 * share), f32),
            ("reduce", "seq", grad_down.astype(b16).reshape(n_seq, part, share), f32),
        ],
    )
    middle_own = lax.dynamic_slice_in_dim(middle, stream * rows, rows, axis=0)
    output = (middle_own + down_sum).astype(b16)
    back_two = norm_backward(
        back_sum.reshape(streams * rows, width).astype(f32), scaled_two, inverse_two, gain_two
    )
    grad_middle = grad_flat.astype(f32) + back_two
    grad_group = grad_middle.astype(b16)
    grad_out_weight = lax.dot_general(
        grad_group, attended_flat, (((0,), (0,)), ((), ())), preferred_element_type=f32
    )
    grad_attended = lax.dot_general(
        grad_group, out_rows, (((1,), (1,)), ((), ())), preferred_element_type=f32
    ).astype(b16)

    def backward_stream(
        stream_query,
        stream_keys,
        stream_values,
        stream_ids,
        stream_key_ids,
        stream_total,
        stream_attended,
        stream_grad,
    ):
        return attention_backward(
            stream_query,
            stream_keys,
            stream_values,
            stream_ids,
            stream_key_ids,
            stream_total,
            stream_attended,
            stream_grad,
            block,
            reach,
        )

    grad_query, keys_acc, values_acc = jax.vmap(backward_stream)(
        query,
        ext_keys,
        ext_values,
        ids_query,
        ids_key,
        log_total,
        attended,
        grad_attended.reshape(streams, rows, heads_here, HEAD),
    )
    rims = jnp.concatenate(
        [keys_acc.reshape(streams, -1, quarter), values_acc.reshape(streams, -1, quarter)], axis=2
    )
    edges = jnp.concatenate([rims[:, :reach], rims[:, -reach:]], axis=1)
    arrived = with_halo(edges.astype(jnp.bfloat16), (("seq", 1),), WIN).astype(edges.dtype)
    owned = (
        rims[:, reach : reach + rows]
        + jnp.pad(arrived[:, :reach], ((0, 0), (0, rows - reach), (0, 0)))
        + jnp.pad(arrived[:, -reach:], ((0, 0), (rows - reach, 0), (0, 0)))
    )
    grad_keys = unrotate(
        owned[:, :, :quarter].reshape(streams, rows, heads_here, HEAD), cosine, sine
    )
    grad_values = owned[:, :, quarter:]
    grad_query = unrotate(grad_query, cosine, sine)
    grad_projected = jnp.concatenate(
        [
            grad_query.reshape(streams * rows, quarter),
            grad_keys.reshape(streams * rows, quarter),
            grad_values.reshape(streams * rows, quarter),
        ],
        axis=1,
    ).astype(jnp.bfloat16)
    grad_qkv = lax.dot_general(
        group_one, grad_projected, (((0,), (0,)), ((), ())), preferred_element_type=f32
    )
    partial_one = lax.dot_general(
        grad_projected, qkv_flat, (((1,), (1,)), ((), ())), preferred_element_type=f32
    )
    grad_gain_one = jnp.sum(partial_one * scaled_one, axis=0)
    gain_parts = jnp.stack([grad_gain_one, grad_gain_two]).reshape(2, n_seq, part)
    gain_parts = jnp.pad(gain_parts.transpose(1, 0, 2), ((0, 0), (0, 6), (0, -part % 128)))
    gain_sums, one_sum, summed_qkv, summed_out = communicate(
        4,
        [
            ("reduce2", "seq", gain_parts, f32),
            ("reduce", "fsdp", partial_one.astype(b16).reshape(streams, rows, width), f32),
            ("reduce", "seq", grad_qkv.astype(b16).reshape(n_seq, part, 3 * quarter), f32),
            ("reduce", "seq", grad_out_weight.astype(b16).reshape(n_seq, part, quarter), f32),
        ],
    )
    gain_sum = lax.dynamic_slice_in_dim(jnp.sum(gain_sums, axis=0), stream * piece, piece, axis=1)

    def own_rows(array):
        return lax.dynamic_slice_in_dim(array, stream * rows, rows, axis=0)

    back_one = norm_backward(one_sum, own_rows(scaled_one), own_rows(inverse_one), gain_one)
    input_grad = own_rows(grad_middle) + back_one
    return (
        output[None],
        input_grad[None],
        gain_sum[0],
        summed_qkv.reshape(part, 3, quarter),
        summed_out.T,
        gain_sum[1],
        summed_in.reshape(part, 2, share),
        summed_down,
    )


def solution(mesh):
    in_specs = (
        P("fsdp", "seq", None),
        P(),
        P(("seq", "fsdp")),
        P("seq", None, "fsdp"),
        P("fsdp", "seq"),
        P(("seq", "fsdp")),
        P("seq", None, "fsdp"),
        P("seq", "fsdp"),
        P("fsdp", "seq", None),
    )
    out_specs = (
        P("fsdp", "seq", None),
        P("fsdp", "seq", None),
        P(("seq", "fsdp")),
        P("seq", None, "fsdp"),
        P("fsdp", "seq"),
        P(("seq", "fsdp")),
        P("seq", None, "fsdp"),
        P("seq", "fsdp"),
    )
    return jax.shard_map(
        per_device, mesh=mesh, in_specs=in_specs, out_specs=out_specs, check_vma=False
    )
```

```python
import functools

import jax
import jax.numpy as jnp
from jax import lax
from jax.experimental import pallas as pl
from jax.experimental.pallas import tpu as pltpu
from jax.sharding import PartitionSpec as P

HEAD = 64
WIN = 64


EPSILON = 1e-05


class Place:
    def __init__(self, axis):
        self.axis = axis
        self.n = lax.axis_size(axis)
        self.length = self.n // 2
        me = lax.axis_index(axis)
        self.me = me
        self.at = me // 2
        self.side = me % 2

    def partner(self):
        return {self.axis: self.at * 2 + (1 - self.side)}

    def right(self):
        return {self.axis: self.me + 2}

    def left(self):
        return {self.axis: self.me - 2}

    def has_right(self):
        return self.at < self.length - 1

    def has_left(self):
        return self.at > 0

    def greet(self, barrier):
        mesh = pl.DeviceIdType.MESH
        pl.semaphore_signal(barrier, inc=1, device_id=self.partner(), device_id_type=mesh)

        @pl.when(self.has_left())
        def _():
            pl.semaphore_signal(barrier, inc=1, device_id=self.left(), device_id_type=mesh)

        @pl.when(self.has_right())
        def _():
            pl.semaphore_signal(barrier, inc=1, device_id=self.right(), device_id_type=mesh)

    def diagonal(self):
        there = jnp.where(self.side == 1, self.has_right(), self.has_left())
        return there, {self.axis: self.me + 2 * self.side - 1}

    def peers(self):
        one, none = jnp.int32(1), jnp.int32(0)
        return 1 + jnp.where(self.has_left(), one, none) + jnp.where(self.has_right(), one, none)


def remote(src, dst, send, recv, device):
    return pltpu.make_async_remote_copy(
        src_ref=src,
        dst_ref=dst,
        send_sem=send,
        recv_sem=recv,
        device_id=device,
        device_id_type=pl.DeviceIdType.MESH,
    )


class Gather:
    scratch = staticmethod(
        lambda n: [
            pltpu.SemaphoreType.DMA((3, n)),
            pltpu.SemaphoreType.DMA((n,)),
            pltpu.SemaphoreType.DMA,
        ]
    )

    def __init__(self, place, src, dst, sems):
        self.place, self.src, self.dst = place, src, dst
        self.send, self.recv, self.local = sems

    def copy(self, way, block, device, own=False):
        src = self.src if own else self.dst.at[block]
        return remote(src, self.dst.at[block], self.send.at[way, block], self.recv.at[block], device)

    def onward(self, block, own, act):
        place = self.place
        act(self.copy(0, block, place.partner(), own))

    def start(self):
        place = self.place
        pltpu.make_async_copy(self.src, self.dst.at[place.me], self.local).start()
        self.ahead(place.me, True, lambda c: c.start())
        self.behind(place.me, True, lambda c: c.start())
        self.onward(place.me, True, lambda c: c.start())

    def ahead(self, block, own, act):
        place = self.place

        @pl.when(place.has_right())
        def _():
            act(self.copy(1, block, place.right(), own))

    def behind(self, block, own, act):
        place = self.place

        @pl.when(place.has_left())
        def _():
            act(self.copy(2, block, place.left(), own))

    def step(self, d):
        place = self.place

        @pl.when(place.at - d >= 0)
        def _():
            block = place.me - 2 * d
            self.copy(1, block, place.partner()).wait_recv()
            self.ahead(block, False, lambda c: c.start())
            self.onward(block, False, lambda c: c.start())

        @pl.when(place.at + d < place.length)
        def _():
            block = place.me + 2 * d
            self.copy(2, block, place.partner()).wait_recv()
            self.behind(block, False, lambda c: c.start())
            self.onward(block, False, lambda c: c.start())

    def finish(self):
        place = self.place
        pltpu.make_async_copy(self.src, self.dst.at[place.me], self.local).wait()

        def arrived(i, carry):
            self.copy(0, 2 * i + 1 - place.side, place.partner()).wait_recv()
            self.onward(2 * i + place.side, False, lambda c: c.wait_send())

            @pl.when(i <= place.at)
            def _():
                self.ahead(2 * i + place.side, False, lambda c: c.wait_send())

            @pl.when(i >= place.at)
            def _():
                self.behind(2 * i + place.side, False, lambda c: c.wait_send())

            return carry

        lax.fori_loop(0, place.length, arrived, 0)


class Reduce:
    @staticmethod
    def scratch(n, block, dtype):
        length = n // 2
        return [
            pltpu.VMEM((length,) + block, dtype),
            pltpu.VMEM((length,) + block, dtype),
            pltpu.VMEM((length + 1,) + block, dtype),
            pltpu.SemaphoreType.DMA((2, length)),
            pltpu.SemaphoreType.DMA((length,)),
            pltpu.SemaphoreType.DMA((length + 1,)),
        ]

    def __init__(self, place, src, dst, scratch):
        self.place, self.src, self.dst = place, src, dst
        self.stage, self.paired, self.lined, self.send, self.pair_recv, self.line_recv = scratch

    def across(self, i):
        place = self.place
        return remote(
            self.src.at[2 * i + 1 - place.side],
            self.paired.at[i],
            self.send.at[0, i],
            self.pair_recv.at[i],
            place.partner(),
        )

    def along(self, i, slot, device):
        return remote(
            self.stage.at[i], self.lined.at[slot], self.send.at[1, i], self.line_recv.at[slot], device
        )

    def start(self):
        place = self.place

        def each(k, carry):
            d = place.length - 1 - k

            @pl.when(place.at + d < place.length)
            def _():
                self.across(place.at + d).start()

            @pl.when(jnp.logical_and(d > 0, place.at - d >= 0))
            def _():
                self.across(place.at - d).start()

            return carry

        lax.fori_loop(0, place.length, each, 0)

    def add(self, out, refs):
        rows = out.shape[0]
        tile = 16 if rows % 16 == 0 else 8

        def each(i, carry):
            at = pl.ds(pl.multiple_of(i * tile, tile), tile)
            total = refs[0][at, :].astype(jnp.float32)
            for ref in refs[1:]:
                total = total + ref[at, :].astype(jnp.float32)
            out[at, :] = total.astype(out.dtype)
            return carry

        lax.fori_loop(0, rows // tile, each, 0)

    def own(self, i):
        self.across(i).wait_recv()
        return [self.src.at[2 * i + self.place.side], self.paired.at[i]]

    def step(self, d):
        place = self.place

        @pl.when(place.at + d < place.length)
        def _():
            i = place.at + d
            refs = self.own(i)

            @pl.when(place.has_left())
            def _():
                self.along(i, i, place.partner()).wait_recv()
                self.add(self.stage.at[i], refs + [self.lined.at[i]])

            @pl.when(jnp.logical_not(place.has_left()))
            def _():
                self.add(self.stage.at[i], refs)

            self.along(i, i, place.right()).start()

        @pl.when(place.at - d >= 0)
        def _():
            i = place.at - d
            refs = self.own(i)

            @pl.when(place.has_right())
            def _():
                self.along(i, i, place.partner()).wait_recv()
                self.add(self.stage.at[i], refs + [self.lined.at[i]])

            @pl.when(jnp.logical_not(place.has_right()))
            def _():
                self.add(self.stage.at[i], refs)

            slot = jnp.where(d == 1, place.length, i)
            self.along(i, slot, place.left()).start()

    def last(self):
        place = self.place
        i, extra = place.at, place.length
        refs = self.own(i)

        @pl.when(place.has_left())
        def _():
            self.along(i, i, place.partner()).wait_recv()

        @pl.when(place.has_right())
        def _():
            self.along(i, extra, place.partner()).wait_recv()

        both = jnp.logical_and(place.has_left(), place.has_right())

        @pl.when(both)
        def _():
            self.add(self.dst, refs + [self.lined.at[i], self.lined.at[extra]])

        @pl.when(jnp.logical_and(place.has_left(), jnp.logical_not(both)))
        def _():
            self.add(self.dst, refs + [self.lined.at[i]])

        @pl.when(jnp.logical_and(place.has_right(), jnp.logical_not(both)))
        def _():
            self.add(self.dst, refs + [self.lined.at[extra]])

    def finish(self):
        place = self.place

        def each(i, carry):
            self.across(i).wait_send()

            @pl.when(i != place.at)
            def _():
                self.along(i, i, place.partner()).wait_send()

            return carry

        lax.fori_loop(0, place.length, each, 0)


class Halo:
    scratch = staticmethod(lambda: [pltpu.SemaphoreType.DMA((2,)), pltpu.SemaphoreType.DMA((2,))])

    def __init__(self, place, src, mid, sems):
        self.place, self.src, self.mid = place, src, mid
        self.send, self.recv = sems
        self.after = place.me < place.n - 1
        self.before = place.me > 0

    def copy(self, way):
        rows, width = self.src.shape[0], self.mid.shape[1]
        at = rows - width if way == 0 else 0
        other = {self.place.axis: self.place.me + 1 - 2 * way}
        return remote(
            self.src.at[pl.ds(at, width)],
            self.mid.at[way],
            self.send.at[way],
            self.recv.at[way],
            other,
        )

    def start(self):
        @pl.when(self.after)
        def _():
            self.copy(0).start()

        @pl.when(self.before)
        def _():
            self.copy(1).start()

        @pl.when(jnp.logical_not(self.before))
        def _():
            self.mid[0] = jnp.zeros(self.mid.shape[1:], self.mid.dtype)

        @pl.when(jnp.logical_not(self.after))
        def _():
            self.mid[1] = jnp.zeros(self.mid.shape[1:], self.mid.dtype)

    def arrive(self):
        @pl.when(self.before)
        def _():
            self.copy(0).wait_recv()

        @pl.when(self.after)
        def _():
            self.copy(1).wait_recv()

    def finish(self):
        @pl.when(self.after)
        def _():
            self.copy(0).wait_send()

        @pl.when(self.before)
        def _():
            self.copy(1).wait_send()


def greet_all(places, slanted):
    barrier = pltpu.get_barrier_semaphore()
    extra = jnp.int32(0)
    if slanted:
        there, device = places[0].diagonal()
        extra = jnp.where(there, jnp.int32(1), jnp.int32(0))

        @pl.when(there)
        def _():
            pl.semaphore_signal(
                barrier, inc=1, device_id=device, device_id_type=pl.DeviceIdType.MESH
            )

    for place in places:
        place.greet(barrier)
    pl.semaphore_wait(barrier, extra + sum(place.peers() for place in places))


def steps(jobs, down, skip=0, stop=None):
    length = jobs[0].place.length
    stop = length - 1 if stop is None else min(stop, length - 1)

    def each(k, carry):
        d = length - 1 - k if down else k + 1
        for job in jobs:
            job.step(d)
        return carry

    if skip < stop:
        lax.fori_loop(skip, stop, each, 0)


def take(items, count):
    return items[:count], items[count:]


def comm_kernel(plan, *refs):
    seq, fsdp = Place("seq"), Place("fsdp")
    places = {"seq": seq, "fsdp": fsdp}
    ins, rest = take(list(refs), len(plan))
    outs, scratch = take(rest, len(plan))
    jobs = []
    for (kind, axis), src, dst in zip(plan, ins, outs):
        place = places.get(axis)
        if kind == "gather":
            own, scratch = take(scratch, 3)
            jobs.append((kind, axis, Gather(place, src, dst, own), None))
        elif kind == "reduce":
            own, scratch = take(scratch, 6)
            jobs.append((kind, axis, Reduce(place, src, dst, own), None))
        elif kind == "sum":
            own, scratch = take(scratch, 6)
            mid, scratch = take(scratch, 1)
            sems, scratch = take(scratch, 3)
            jobs.append((kind, axis, Reduce(place, src, mid[0], own), Gather(place, mid[0], dst, sems)))
        elif kind == "gather2":
            own, scratch = take(scratch, 3)
            mid, scratch = take(scratch, 1)
            sems, scratch = take(scratch, 3)
            jobs.append((kind, axis, Gather(seq, src, mid[0], own), Gather(fsdp, mid[0], dst, sems)))
        elif kind == "reduce2":
            own, scratch = take(scratch, 6)
            mid, scratch = take(scratch, 1)
            sems, scratch = take(scratch, 3)
            jobs.append((kind, axis, Reduce(seq, src, mid[0], own), Gather(fsdp, mid[0], dst, sems)))
        elif kind == "halo":
            sems, scratch = take(scratch, 2)
            mid, scratch = take(scratch, 1)
            own, scratch = take(scratch, 3)
            jobs.append((kind, axis, Halo(seq, src, mid[0], sems), Gather(fsdp, mid[0], dst, own)))
    ga = [j for k, a, j, _ in jobs if a == "seq" and isinstance(j, Gather)]
    gb = [j for k, a, j, _ in jobs if a == "fsdp" and isinstance(j, Gather)]
    ra = [j for k, a, j, _ in jobs if a == "seq" and isinstance(j, Reduce)]
    rb = [j for k, a, j, _ in jobs if a == "fsdp" and isinstance(j, Reduce)]
    halos = [j for k, a, j, _ in jobs if k == "halo"]
    rims = [j for k, a, _, j in jobs if k == "halo"]
    second = [j for k, a, _, j in jobs if k == "sum"]
    late = [j for k, a, _, j in jobs if k in ("gather2", "reduce2")]
    greet_all((seq, fsdp), bool(halos))
    for job in halos + rb + ra + gb + ga:
        job.start()
    for job in halos:
        job.arrive()
    for job in rims:
        job.start()
    if rb:
        steps(rb, True)
    if ra:
        steps(ra, True, stop=1)
    for job in rb:
        job.last()
    for job in second:
        job.start()
    if ga:
        steps(ga, False)
    if gb:
        steps(gb + rims, False)
    if ra:
        steps(ra, True, skip=1)
    for job in ra:
        job.last()
    if second:
        steps(second, False)
    for job in ga:
        job.finish()
    for job in late:
        job.start()
    if late:
        steps(late, False)
    for job in halos + rims + gb + rb + ra + second + late:
        job.finish()


def communicate(number, jobs):
    sizes = {axis: lax.axis_size(axis) for axis in ("seq", "fsdp")}
    shapes, scratch = [], []
    for kind, axis, array, dtype in jobs:
        n = sizes.get(axis)
        if kind == "gather":
            shapes.append((n,) + array.shape)
            scratch += Gather.scratch(n)
        elif kind == "halo":
            mid = (2, WIN, array.shape[1])
            shapes.append((sizes["fsdp"],) + mid)
            scratch += Halo.scratch() + [pltpu.VMEM(mid, array.dtype)]
            scratch += Gather.scratch(sizes["fsdp"])
        elif kind == "gather2":
            shapes.append((sizes["fsdp"], n) + array.shape)
            scratch += Gather.scratch(n)
            scratch += [pltpu.VMEM((n,) + array.shape, array.dtype)] + Gather.scratch(sizes["fsdp"])
        else:
            block = array.shape[1:]
            scratch += Reduce.scratch(n, block, array.dtype)
            if kind == "reduce":
                shapes.append(block)
            elif kind == "sum":
                shapes.append(array.shape)
                scratch += [pltpu.VMEM(block, dtype)] + Gather.scratch(n)
            else:
                shapes.append((sizes["fsdp"],) + block)
                scratch += [pltpu.VMEM(block, dtype)] + Gather.scratch(sizes["fsdp"])
    vmem = pl.BlockSpec(memory_space=pltpu.VMEM)
    return pl.pallas_call(
        functools.partial(comm_kernel, tuple((kind, axis) for kind, axis, _, _ in jobs)),
        out_shape=[jax.ShapeDtypeStruct(s, j[3]) for s, j in zip(shapes, jobs)],
        in_specs=[vmem] * len(jobs),
        out_specs=[vmem] * len(jobs),
        scratch_shapes=scratch,
        compiler_params=pltpu.CompilerParams(
            collective_id=number, has_side_effects=True, vmem_limit_bytes=60 * 1024 * 1024
        ),
    )(*[array for _, _, array, _ in jobs])


def with_halo(value, sides, width):
    for axis, dim in sides:
        devices, length = (lax.axis_size(axis), value.shape[dim])
        up = [(i, (i + 1) % devices) for i in range(devices - 1)]
        down = [(j, i) for i, j in up]
        last = lax.slice_in_dim(value, length - width, length, axis=dim)
        first = lax.slice_in_dim(value, 0, width, axis=dim)
        before = lax.ppermute(last, axis, up)
        after = lax.ppermute(first, axis, down)
        value = jnp.concatenate([before, value, after], axis=dim)
    return value


def norm_forward(values, gain):
    mean = jnp.mean(values, axis=-1, keepdims=True)
    centred = values - mean
    inverse = lax.rsqrt(jnp.mean(centred * centred, axis=-1, keepdims=True) + EPSILON)
    scaled = centred * inverse
    return (scaled, inverse, (scaled * gain.astype(jnp.float32)).astype(jnp.bfloat16))


def norm_backward(grad, scaled, inverse, gain):
    weighted = grad * gain.astype(jnp.float32)
    back = inverse * (
        weighted
        - jnp.mean(weighted, axis=-1, keepdims=True)
        - scaled * jnp.mean(weighted * scaled, axis=-1, keepdims=True)
    )
    return back


def gelu_parts(inner):
    cdf = 0.5 * (1.0 + jax.scipy.special.erf(inner * 0.7071067811865476))
    density = jnp.exp(-0.5 * inner * inner) * 0.3989422804014327
    return (inner * cdf, cdf + inner * density)


def rope_tables(positions, head_size):
    half = head_size // 2
    inv_freq = 10000.0 ** (-(2.0 / head_size) * jnp.arange(half, dtype=jnp.float32))
    angle = positions.astype(jnp.float32)[:, None] * inv_freq[None, :]
    return (jnp.cos(angle)[:, None, :], jnp.sin(angle)[:, None, :])


def rotate(field, cosine, sine):
    half = field.shape[-1] // 2
    first, second = (field[..., :half], field[..., half:])
    return jnp.concatenate(
        [first * cosine - second * sine, second * cosine + first * sine], axis=-1
    )


def unrotate(grad, cosine, sine):
    half = grad.shape[-1] // 2
    first, second = (grad[..., :half], grad[..., half:])
    return jnp.concatenate(
        [first * cosine + second * sine, second * cosine - first * sine], axis=-1
    )


def doc_ids(lengths_row, positions):
    starts = jnp.cumsum(lengths_row, dtype=jnp.int32) - lengths_row
    total = jnp.sum(lengths_row, dtype=jnp.int32)
    found = (
        jnp.sum((positions[:, None] >= starts[None, :]).astype(jnp.int32), axis=1, dtype=jnp.int32)
        - 1
    )
    valid = (positions >= 0) & (positions < total)
    return jnp.where(valid, found, -1)


def window_mask(ids_query, ids_key, reach):
    block = ids_query.shape[0]
    offset = (
        jnp.arange(block, dtype=jnp.int32)[:, None]
        + reach
        - jnp.arange(block + 2 * reach, dtype=jnp.int32)[None, :]
    )
    return (jnp.abs(offset) <= reach) & (ids_query[:, None] == ids_key[None, :])


def attend_forward(query, keys, values, allowed):
    scale = query.shape[-1] ** (-0.5)
    scores = jnp.einsum("nhe,mhe->hnm", query, keys, preferred_element_type=jnp.float32) * scale
    masked = jnp.where(allowed[None], scores, -1e30)
    top = jnp.max(masked, axis=-1, keepdims=True)
    expd = jnp.exp(masked - top)
    total = jnp.sum(expd, axis=-1, keepdims=True)
    log_total = (top + jnp.log(total))[..., 0]
    probs = (expd / total).astype(jnp.bfloat16)
    out = jnp.einsum("hnm,mhe->nhe", probs, values, preferred_element_type=jnp.float32)
    return (out.astype(jnp.bfloat16), log_total)


def attend_backward(query, keys, values, allowed, log_total, attended, grad_out):
    scale = query.shape[-1] ** (-0.5)
    scores = jnp.einsum("nhe,mhe->hnm", query, keys, preferred_element_type=jnp.float32) * scale
    masked = jnp.where(allowed[None], scores, -1e30)
    again = jnp.exp(masked - log_total[..., None])
    again_b = again.astype(jnp.bfloat16)
    grad_values = jnp.einsum("hnm,nhe->mhe", again_b, grad_out, preferred_element_type=jnp.float32)
    grad_probs = jnp.einsum("nhe,mhe->hnm", grad_out, values, preferred_element_type=jnp.float32)
    delta = jnp.sum(grad_out.astype(jnp.float32) * attended.astype(jnp.float32), axis=-1).T
    grad_scores = (again * (grad_probs - delta[..., None]) * scale).astype(jnp.bfloat16)
    grad_query = jnp.einsum("hnm,mhe->nhe", grad_scores, keys, preferred_element_type=jnp.float32)
    grad_keys = jnp.einsum("hnm,nhe->mhe", grad_scores, query, preferred_element_type=jnp.float32)
    return (grad_query, grad_keys, grad_values)


def attention_forward(query, ext_keys, ext_values, ids_query, ids_key, block, reach):
    rows, heads = (query.shape[0], query.shape[1])
    count = rows // block

    def step(carry, index):
        allowed = window_mask(ids_query, ids_key, reach)
        return (carry, attend_forward(query, ext_keys, ext_values, allowed))

    _, (outs, totals) = lax.scan(
        step, jnp.zeros((), jnp.float32), jnp.arange(count, dtype=jnp.int32)
    )
    return (outs.reshape(rows, heads, -1), totals.transpose(1, 0, 2).reshape(heads, rows))


def attention_backward(
    query, ext_keys, ext_values, ids_query, ids_key, log_total, attended, grad_out, block, reach
):
    rows = query.shape[0]
    count = rows // block
    zero = jnp.zeros(ext_keys.shape, jnp.float32)

    def step(carry, index):
        keys_acc, values_acc = carry
        allowed = window_mask(ids_query, ids_key, reach)
        grad_query, grad_keys, grad_values = attend_backward(
            query, ext_keys, ext_values, allowed, log_total, attended, grad_out
        )
        keys_acc = keys_acc + grad_keys
        values_acc = values_acc + grad_values
        return ((keys_acc, values_acc), grad_query)

    (keys_acc, values_acc), grads = lax.scan(step, (zero, zero), jnp.arange(count, dtype=jnp.int32))
    return (grads.reshape(query.shape), keys_acc, values_acc)


def per_device(
    layer_input,
    doc_lengths,
    attn_gain,
    qkv_weight,
    out_weight,
    mlp_gain,
    in_weight,
    down_weight,
    out_grad,
):
    tokens = layer_input[0]
    grad_rows = out_grad[0]
    rows, width = tokens.shape
    streams = doc_lengths.shape[0]
    quarter = qkv_weight.shape[2]
    heads_here = quarter // HEAD
    share = down_weight.shape[1]
    reach = WIN
    block = min(rows, 512)
    n_seq, n_fsdp = lax.axis_size("seq"), lax.axis_size("fsdp")
    stream = lax.axis_index("fsdp")
    part = width // n_seq
    piece = attn_gain.shape[0]
    b16, f32 = jnp.bfloat16, jnp.float32
    first = lax.axis_index("seq") * rows
    positions = first + jnp.arange(rows, dtype=jnp.int32)
    outer = first - reach + jnp.arange(rows + 2 * reach, dtype=jnp.int32)
    ids_query = jax.vmap(doc_ids, in_axes=(0, None))(doc_lengths, positions)
    ids_key = jax.vmap(doc_ids, in_axes=(0, None))(doc_lengths, outer)
    cosine, sine = rope_tables(positions, HEAD)
    gains = jnp.pad(jnp.stack([attn_gain, mlp_gain]), ((0, 14), (0, 128 - piece)))
    gains_all, rim_all, tokens_all, grad_all, qkv_all, out_all = communicate(
        1,
        [
            ("gather2", "seq", gains, b16),
            ("halo", "both", tokens, b16),
            ("gather", "fsdp", tokens, b16),
            ("gather", "fsdp", grad_rows, b16),
            ("gather", "seq", qkv_weight.reshape(part, 3 * quarter), b16),
            ("gather", "seq", out_weight, b16),
        ],
    )
    gain_one = gains_all[:, :, 0, :piece].transpose(1, 0, 2).reshape(width)
    gain_two = gains_all[:, :, 1, :piece].transpose(1, 0, 2).reshape(width)
    qkv_flat = qkv_all.reshape(width, 3 * quarter)
    out_rows = out_all.transpose(1, 0, 2).reshape(quarter, width)
    grad_flat = grad_all.reshape(streams * rows, width)
    resid_in = tokens_all.reshape(streams * rows, width).astype(f32)
    scaled_one, inverse_one, group_one = norm_forward(resid_in, gain_one)
    rim_rows = streams * 2 * reach
    normed_rim = norm_forward(rim_all.reshape(rim_rows, width).astype(f32), gain_one)[2]
    normed_rim = normed_rim.reshape(streams, 2, reach, width)
    normed_outer = jnp.concatenate(
        [normed_rim[:, 0], group_one.reshape(streams, rows, width), normed_rim[:, 1]], axis=1
    ).reshape(streams * (rows + 2 * reach), width)
    outer_cosine, outer_sine = rope_tables(outer, HEAD)
    projected = jnp.dot(group_one, qkv_flat[:, :quarter], preferred_element_type=f32)
    query = rotate(projected.reshape(streams, rows, heads_here, HEAD), cosine, sine).astype(b16)
    projected = jnp.dot(normed_outer, qkv_flat[:, quarter:], preferred_element_type=f32)
    split = projected.reshape(streams, rows + 2 * reach, 2, heads_here, HEAD)
    ext_keys = rotate(split[:, :, 0], outer_cosine, outer_sine).astype(b16)
    ext_values = split[:, :, 1].astype(b16)

    def forward_stream(stream_query, stream_keys, stream_values, stream_ids, stream_key_ids):
        return attention_forward(
            stream_query, stream_keys, stream_values, stream_ids, stream_key_ids, block, reach
        )

    attended, log_total = jax.vmap(forward_stream)(query, ext_keys, ext_values, ids_query, ids_key)
    attended_flat = attended.reshape(streams * rows, quarter)
    partial_attn = jnp.dot(attended_flat, out_rows, preferred_element_type=f32)
    attn_sum, in_all, down_all = communicate(
        2,
        [
            ("sum", "fsdp", partial_attn.astype(b16).reshape(streams, rows, width), b16),
            ("gather", "seq", in_weight.reshape(part, 2 * share), b16),
            ("gather", "seq", down_weight, b16),
        ],
    )
    in_flat = in_all.reshape(width, 2 * share)
    down_full = down_all.reshape(width, share)
    middle = resid_in + attn_sum.reshape(streams * rows, width).astype(f32)
    scaled_two, inverse_two, normed_flat = norm_forward(middle, gain_two)
    hidden = jnp.dot(normed_flat, in_flat, preferred_element_type=f32)
    inner, gate = (hidden[:, :share], hidden[:, share:])
    activated, slope = gelu_parts(inner)
    mixed = (activated * gate).astype(b16)
    partial_down = lax.dot_general(
        mixed, down_full, (((1,), (1,)), ((), ())), preferred_element_type=f32
    )
    grad_down = lax.dot_general(
        grad_flat, mixed, (((0,), (0,)), ((), ())), preferred_element_type=f32
    )
    grad_mixed = jnp.dot(grad_flat, down_full, preferred_element_type=f32)
    grad_hidden = jnp.concatenate(
        [grad_mixed * gate * slope, grad_mixed * activated], axis=1
    ).astype(b16)
    grad_in = lax.dot_general(
        normed_flat, grad_hidden, (((0,), (0,)), ((), ())), preferred_element_type=f32
    )
    partial_back = lax.dot_general(
        grad_hidden, in_flat, (((1,), (1,)), ((), ())), preferred_element_type=f32
    )
    grad_gain_two = jnp.sum(partial_back * scaled_two, axis=0)
    back_sum, down_sum, summed_in, summed_down = communicate(
        3,
        [
            ("sum", "fsdp", partial_back.astype(b16).reshape(streams, rows, width), b16),
            ("reduce", "fsdp", partial_down.astype(b16).reshape(streams, rows, width), f32),
            ("reduce", "seq", grad_in.astype(b16).reshape(n_seq, part, 2 * share), f32),
            ("reduce", "seq", grad_down.astype(b16).reshape(n_seq, part, share), f32),
        ],
    )
    middle_own = lax.dynamic_slice_in_dim(middle, stream * rows, rows, axis=0)
    output = (middle_own + down_sum).astype(b16)
    back_two = norm_backward(
        back_sum.reshape(streams * rows, width).astype(f32), scaled_two, inverse_two, gain_two
    )
    grad_middle = grad_flat.astype(f32) + back_two
    grad_group = grad_middle.astype(b16)
    grad_out_weight = lax.dot_general(
        grad_group, attended_flat, (((0,), (0,)), ((), ())), preferred_element_type=f32
    )
    grad_attended = lax.dot_general(
        grad_group, out_rows, (((1,), (1,)), ((), ())), preferred_element_type=f32
    ).astype(b16)

    def backward_stream(
        stream_query,
        stream_keys,
        stream_values,
        stream_ids,
        stream_key_ids,
        stream_total,
        stream_attended,
        stream_grad,
    ):
        return attention_backward(
            stream_query,
            stream_keys,
            stream_values,
            stream_ids,
            stream_key_ids,
            stream_total,
            stream_attended,
            stream_grad,
            block,
            reach,
        )

    grad_query, keys_acc, values_acc = jax.vmap(backward_stream)(
        query,
        ext_keys,
        ext_values,
        ids_query,
        ids_key,
        log_total,
        attended,
        grad_attended.reshape(streams, rows, heads_here, HEAD),
    )
    rims = jnp.concatenate(
        [keys_acc.reshape(streams, -1, quarter), values_acc.reshape(streams, -1, quarter)], axis=2
    )
    edges = jnp.concatenate([rims[:, :reach], rims[:, -reach:]], axis=1)
    arrived = with_halo(edges.astype(jnp.bfloat16), (("seq", 1),), WIN).astype(edges.dtype)
    owned = (
        rims[:, reach : reach + rows]
        + jnp.pad(arrived[:, :reach], ((0, 0), (0, rows - reach), (0, 0)))
        + jnp.pad(arrived[:, -reach:], ((0, 0), (rows - reach, 0), (0, 0)))
    )
    grad_keys = unrotate(
        owned[:, :, :quarter].reshape(streams, rows, heads_here, HEAD), cosine, sine
    )
    grad_values = owned[:, :, quarter:]
    grad_query = unrotate(grad_query, cosine, sine)
    grad_projected = jnp.concatenate(
        [
            grad_query.reshape(streams * rows, quarter),
            grad_keys.reshape(streams * rows, quarter),
            grad_values.reshape(streams * rows, quarter),
        ],
        axis=1,
    ).astype(jnp.bfloat16)
    grad_qkv = lax.dot_general(
        group_one, grad_projected, (((0,), (0,)), ((), ())), preferred_element_type=f32
    )
    partial_one = lax.dot_general(
        grad_projected, qkv_flat, (((1,), (1,)), ((), ())), preferred_element_type=f32
    )
    grad_gain_one = jnp.sum(partial_one * scaled_one, axis=0)
    gain_parts = jnp.stack([grad_gain_one, grad_gain_two]).reshape(2, n_seq, part)
    gain_parts = jnp.pad(gain_parts.transpose(1, 0, 2), ((0, 0), (0, 6), (0, -part % 128)))
    gain_sums, one_sum, summed_qkv, summed_out = communicate(
        4,
        [
            ("reduce2", "seq", gain_parts, f32),
            ("reduce", "fsdp", partial_one.astype(b16).reshape(streams, rows, width), f32),
            ("reduce", "seq", grad_qkv.astype(b16).reshape(n_seq, part, 3 * quarter), f32),
            ("reduce", "seq", grad_out_weight.astype(b16).reshape(n_seq, part, quarter), f32),
        ],
    )
    gain_sum = lax.dynamic_slice_in_dim(jnp.sum(gain_sums, axis=0), stream * piece, piece, axis=1)

    def own_rows(array):
        return lax.dynamic_slice_in_dim(array, stream * rows, rows, axis=0)

    back_one = norm_backward(one_sum, own_rows(scaled_one), own_rows(inverse_one), gain_one)
    input_grad = own_rows(grad_middle) + back_one
    return (
        output[None],
        input_grad[None],
        gain_sum[0],
        summed_qkv.reshape(part, 3, quarter),
        summed_out.T,
        gain_sum[1],
        summed_in.reshape(part, 2, share),
        summed_down,
    )


def solution(mesh):
    in_specs = (
        P("fsdp", "seq", None),
        P(),
        P(("seq", "fsdp")),
        P("seq", None, "fsdp"),
        P("fsdp", "seq"),
        P(("seq", "fsdp")),
        P("seq", None, "fsdp"),
        P("seq", "fsdp"),
        P("fsdp", "seq", None),
    )
    out_specs = (
        P("fsdp", "seq", None),
        P("fsdp", "seq", None),
        P(("seq", "fsdp")),
        P("seq", None, "fsdp"),
        P("fsdp", "seq"),
        P(("seq", "fsdp")),
        P("seq", None, "fsdp"),
        P("seq", "fsdp"),
    )
    return jax.shard_map(
        per_device, mesh=mesh, in_specs=in_specs, out_specs=out_specs, check_vma=False
    )
```

```python
import functools

import jax
import jax.numpy as jnp
from jax import lax
from jax.experimental import pallas as pl
from jax.experimental.pallas import tpu as pltpu
from jax.sharding import PartitionSpec as P

HEAD = 64
WIN = 64


EPSILON = 1e-05


class Place:
    def __init__(self, axis):
        self.axis = axis
        self.n = lax.axis_size(axis)
        self.length = self.n // 2
        me = lax.axis_index(axis)
        self.me = me
        self.at = me // 2
        self.side = me % 2

    def partner(self):
        return {self.axis: self.at * 2 + (1 - self.side)}

    def right(self):
        return {self.axis: self.me + 2}

    def left(self):
        return {self.axis: self.me - 2}

    def has_right(self):
        return self.at < self.length - 1

    def has_left(self):
        return self.at > 0

    def greet(self, barrier):
        mesh = pl.DeviceIdType.MESH
        pl.semaphore_signal(barrier, inc=1, device_id=self.partner(), device_id_type=mesh)

        @pl.when(self.has_left())
        def _():
            pl.semaphore_signal(barrier, inc=1, device_id=self.left(), device_id_type=mesh)

        @pl.when(self.has_right())
        def _():
            pl.semaphore_signal(barrier, inc=1, device_id=self.right(), device_id_type=mesh)

    def diagonal(self):
        there = jnp.where(self.side == 1, self.has_right(), self.has_left())
        return there, {self.axis: self.me + 2 * self.side - 1}

    def peers(self):
        one, none = jnp.int32(1), jnp.int32(0)
        return 1 + jnp.where(self.has_left(), one, none) + jnp.where(self.has_right(), one, none)


def remote(src, dst, send, recv, device):
    return pltpu.make_async_remote_copy(
        src_ref=src,
        dst_ref=dst,
        send_sem=send,
        recv_sem=recv,
        device_id=device,
        device_id_type=pl.DeviceIdType.MESH,
    )


class Gather:
    scratch = staticmethod(
        lambda n: [
            pltpu.SemaphoreType.DMA((3, n)),
            pltpu.SemaphoreType.DMA((n,)),
            pltpu.SemaphoreType.DMA,
        ]
    )

    def __init__(self, place, src, dst, sems):
        self.place, self.src, self.dst = place, src, dst
        self.send, self.recv, self.local = sems

    def copy(self, way, block, device, own=False):
        src = self.src if own else self.dst.at[block]
        return remote(src, self.dst.at[block], self.send.at[way, block], self.recv.at[block], device)

    def onward(self, block, own, act):
        place = self.place
        act(self.copy(0, block, place.partner(), own))

    def start(self):
        place = self.place
        pltpu.make_async_copy(self.src, self.dst.at[place.me], self.local).start()
        self.ahead(place.me, True, lambda c: c.start())
        self.behind(place.me, True, lambda c: c.start())
        self.onward(place.me, True, lambda c: c.start())

    def ahead(self, block, own, act):
        place = self.place

        @pl.when(place.has_right())
        def _():
            act(self.copy(1, block, place.right(), own))

    def behind(self, block, own, act):
        place = self.place

        @pl.when(place.has_left())
        def _():
            act(self.copy(2, block, place.left(), own))

    def step(self, d):
        place = self.place

        @pl.when(place.at - d >= 0)
        def _():
            block = place.me - 2 * d
            self.copy(1, block, place.partner()).wait_recv()
            self.ahead(block, False, lambda c: c.start())
            self.onward(block, False, lambda c: c.start())

        @pl.when(place.at + d < place.length)
        def _():
            block = place.me + 2 * d
            self.copy(2, block, place.partner()).wait_recv()
            self.behind(block, False, lambda c: c.start())
            self.onward(block, False, lambda c: c.start())

    def finish(self):
        place = self.place
        pltpu.make_async_copy(self.src, self.dst.at[place.me], self.local).wait()

        def arrived(i, carry):
            self.copy(0, 2 * i + 1 - place.side, place.partner()).wait_recv()
            self.onward(2 * i + place.side, False, lambda c: c.wait_send())

            @pl.when(i <= place.at)
            def _():
                self.ahead(2 * i + place.side, False, lambda c: c.wait_send())

            @pl.when(i >= place.at)
            def _():
                self.behind(2 * i + place.side, False, lambda c: c.wait_send())

            return carry

        lax.fori_loop(0, place.length, arrived, 0)


class Reduce:
    @staticmethod
    def scratch(n, block, dtype):
        length = n // 2
        return [
            pltpu.VMEM((length,) + block, dtype),
            pltpu.VMEM((length,) + block, dtype),
            pltpu.VMEM((length + 1,) + block, dtype),
            pltpu.SemaphoreType.DMA((2, length)),
            pltpu.SemaphoreType.DMA((length,)),
            pltpu.SemaphoreType.DMA((length + 1,)),
        ]

    def __init__(self, place, src, dst, scratch):
        self.place, self.src, self.dst = place, src, dst
        self.stage, self.paired, self.lined, self.send, self.pair_recv, self.line_recv = scratch

    def across(self, i):
        place = self.place
        return remote(
            self.src.at[2 * i + 1 - place.side],
            self.paired.at[i],
            self.send.at[0, i],
            self.pair_recv.at[i],
            place.partner(),
        )

    def along(self, i, slot, device):
        return remote(
            self.stage.at[i], self.lined.at[slot], self.send.at[1, i], self.line_recv.at[slot], device
        )

    def exchange(self, d):
        place = self.place

        @pl.when(place.at + d < place.length)
        def _():
            self.across(place.at + d).start()

        @pl.when(jnp.logical_and(d > 0, place.at - d >= 0))
        def _():
            self.across(place.at - d).start()

    def add(self, out, refs):
        rows = out.shape[0]
        tile = 16 if rows % 16 == 0 else 8

        def each(i, carry):
            at = pl.ds(pl.multiple_of(i * tile, tile), tile)
            total = refs[0][at, :].astype(jnp.float32)
            for ref in refs[1:]:
                total = total + ref[at, :].astype(jnp.float32)
            out[at, :] = total.astype(out.dtype)
            return carry

        lax.fori_loop(0, rows // tile, each, 0)

    def own(self, i):
        self.across(i).wait_recv()
        return [self.src.at[2 * i + self.place.side], self.paired.at[i]]

    def step(self, d):
        place = self.place

        @pl.when(place.at + d < place.length)
        def _():
            i = place.at + d
            refs = self.own(i)

            @pl.when(place.has_left())
            def _():
                self.along(i, i, place.partner()).wait_recv()
                self.add(self.stage.at[i], refs + [self.lined.at[i]])

            @pl.when(jnp.logical_not(place.has_left()))
            def _():
                self.add(self.stage.at[i], refs)

            self.along(i, i, place.right()).start()

        @pl.when(place.at - d >= 0)
        def _():
            i = place.at - d
            refs = self.own(i)

            @pl.when(place.has_right())
            def _():
                self.along(i, i, place.partner()).wait_recv()
                self.add(self.stage.at[i], refs + [self.lined.at[i]])

            @pl.when(jnp.logical_not(place.has_right()))
            def _():
                self.add(self.stage.at[i], refs)

            slot = jnp.where(d == 1, place.length, i)
            self.along(i, slot, place.left()).start()

    def last(self):
        place = self.place
        i, extra = place.at, place.length
        refs = self.own(i)

        @pl.when(place.has_left())
        def _():
            self.along(i, i, place.partner()).wait_recv()

        @pl.when(place.has_right())
        def _():
            self.along(i, extra, place.partner()).wait_recv()

        both = jnp.logical_and(place.has_left(), place.has_right())

        @pl.when(both)
        def _():
            self.add(self.dst, refs + [self.lined.at[i], self.lined.at[extra]])

        @pl.when(jnp.logical_and(place.has_left(), jnp.logical_not(both)))
        def _():
            self.add(self.dst, refs + [self.lined.at[i]])

        @pl.when(jnp.logical_and(place.has_right(), jnp.logical_not(both)))
        def _():
            self.add(self.dst, refs + [self.lined.at[extra]])

    def finish(self):
        place = self.place

        def each(i, carry):
            self.across(i).wait_send()

            @pl.when(i != place.at)
            def _():
                self.along(i, i, place.partner()).wait_send()

            return carry

        lax.fori_loop(0, place.length, each, 0)


class Halo:
    scratch = staticmethod(lambda: [pltpu.SemaphoreType.DMA((2,)), pltpu.SemaphoreType.DMA((2,))])

    def __init__(self, place, src, mid, sems):
        self.place, self.src, self.mid = place, src, mid
        self.send, self.recv = sems
        self.after = place.me < place.n - 1
        self.before = place.me > 0

    def copy(self, way):
        rows, width = self.src.shape[0], self.mid.shape[1]
        at = rows - width if way == 0 else 0
        other = {self.place.axis: self.place.me + 1 - 2 * way}
        return remote(
            self.src.at[pl.ds(at, width)],
            self.mid.at[way],
            self.send.at[way],
            self.recv.at[way],
            other,
        )

    def start(self):
        @pl.when(self.after)
        def _():
            self.copy(0).start()

        @pl.when(self.before)
        def _():
            self.copy(1).start()

        @pl.when(jnp.logical_not(self.before))
        def _():
            self.mid[0] = jnp.zeros(self.mid.shape[1:], self.mid.dtype)

        @pl.when(jnp.logical_not(self.after))
        def _():
            self.mid[1] = jnp.zeros(self.mid.shape[1:], self.mid.dtype)

    def arrive(self):
        @pl.when(self.before)
        def _():
            self.copy(0).wait_recv()

        @pl.when(self.after)
        def _():
            self.copy(1).wait_recv()

    def finish(self):
        @pl.when(self.after)
        def _():
            self.copy(0).wait_send()

        @pl.when(self.before)
        def _():
            self.copy(1).wait_send()


def greet_all(places, slanted):
    barrier = pltpu.get_barrier_semaphore()
    extra = jnp.int32(0)
    if slanted:
        there, device = places[0].diagonal()
        extra = jnp.where(there, jnp.int32(1), jnp.int32(0))

        @pl.when(there)
        def _():
            pl.semaphore_signal(
                barrier, inc=1, device_id=device, device_id_type=pl.DeviceIdType.MESH
            )

    for place in places:
        place.greet(barrier)
    pl.semaphore_wait(barrier, extra + sum(place.peers() for place in places))


def steps(jobs, down, skip=0, stop=None):
    length = jobs[0].place.length
    stop = length - 1 if stop is None else min(stop, length - 1)

    def each(k, carry):
        d = length - 1 - k if down else k + 1
        for job in jobs:
            job.step(d)
        return carry

    if skip < stop:
        lax.fori_loop(skip, stop, each, 0)


def exchanges(jobs):
    length = jobs[0].place.length

    def each(k, carry):
        for job in jobs:
            job.exchange(length - 1 - k)
        return carry

    lax.fori_loop(0, length, each, 0)


def take(items, count):
    return items[:count], items[count:]


def comm_kernel(plan, *refs):
    seq, fsdp = Place("seq"), Place("fsdp")
    places = {"seq": seq, "fsdp": fsdp}
    ins, rest = take(list(refs), len(plan))
    outs, scratch = take(rest, len(plan))
    jobs = []
    for (kind, axis), src, dst in zip(plan, ins, outs):
        place = places.get(axis)
        if kind == "gather":
            own, scratch = take(scratch, 3)
            jobs.append((kind, axis, Gather(place, src, dst, own), None))
        elif kind == "reduce":
            own, scratch = take(scratch, 6)
            jobs.append((kind, axis, Reduce(place, src, dst, own), None))
        elif kind == "sum":
            own, scratch = take(scratch, 6)
            mid, scratch = take(scratch, 1)
            sems, scratch = take(scratch, 3)
            jobs.append((kind, axis, Reduce(place, src, mid[0], own), Gather(place, mid[0], dst, sems)))
        elif kind == "gather2":
            own, scratch = take(scratch, 3)
            mid, scratch = take(scratch, 1)
            sems, scratch = take(scratch, 3)
            jobs.append((kind, axis, Gather(seq, src, mid[0], own), Gather(fsdp, mid[0], dst, sems)))
        elif kind == "reduce2":
            own, scratch = take(scratch, 6)
            mid, scratch = take(scratch, 1)
            sems, scratch = take(scratch, 3)
            jobs.append((kind, axis, Reduce(seq, src, mid[0], own), Gather(fsdp, mid[0], dst, sems)))
        elif kind == "halo":
            sems, scratch = take(scratch, 2)
            mid, scratch = take(scratch, 1)
            own, scratch = take(scratch, 3)
            jobs.append((kind, axis, Halo(seq, src, mid[0], sems), Gather(fsdp, mid[0], dst, own)))
    ga = [j for k, a, j, _ in jobs if a == "seq" and isinstance(j, Gather)]
    gb = [j for k, a, j, _ in jobs if a == "fsdp" and isinstance(j, Gather)]
    ra = [j for k, a, j, _ in jobs if a == "seq" and isinstance(j, Reduce)]
    rb = [j for k, a, j, _ in jobs if a == "fsdp" and isinstance(j, Reduce)]
    halos = [j for k, a, j, _ in jobs if k == "halo"]
    rims = [j for k, a, _, j in jobs if k == "halo"]
    second = [j for k, a, _, j in jobs if k == "sum"]
    late = [j for k, a, _, j in jobs if k in ("gather2", "reduce2")]
    greet_all((seq, fsdp), bool(halos))
    for job in halos + gb + ga:
        job.start()
    for group in (rb, ra):
        if group:
            exchanges(group)
    for job in halos:
        job.arrive()
    for job in rims:
        job.start()
    if rb:
        steps(rb, True)
    if ra:
        steps(ra, True, stop=1)
    for job in rb:
        job.last()
    for job in second:
        job.start()
    if ga:
        steps(ga, False)
    if gb:
        steps(gb + rims, False)
    if ra:
        steps(ra, True, skip=1)
    for group, act in ((ga, Gather.finish), (ra, Reduce.last)):
        early = [j for k, _, j, _ in jobs if k in ("gather2", "reduce2") and j in group]
        for job in early:
            act(job)
        if early:
            for job in late:
                job.start()
    if second:
        steps(second, False)
    early = [j for k, _, j, _ in jobs if k in ("gather2", "reduce2")]
    for job in ra:
        if job not in early:
            job.last()
    if late:
        steps(late, False)
    for job in ga:
        if job not in early:
            job.finish()
    for job in halos + rims + gb + rb + ra + second + late:
        job.finish()


def communicate(number, jobs):
    sizes = {axis: lax.axis_size(axis) for axis in ("seq", "fsdp")}
    shapes, scratch = [], []
    for kind, axis, array, dtype in jobs:
        n = sizes.get(axis)
        if kind == "gather":
            shapes.append((n,) + array.shape)
            scratch += Gather.scratch(n)
        elif kind == "halo":
            mid = (2, WIN, array.shape[1])
            shapes.append((sizes["fsdp"],) + mid)
            scratch += Halo.scratch() + [pltpu.VMEM(mid, array.dtype)]
            scratch += Gather.scratch(sizes["fsdp"])
        elif kind == "gather2":
            shapes.append((sizes["fsdp"], n) + array.shape)
            scratch += Gather.scratch(n)
            scratch += [pltpu.VMEM((n,) + array.shape, array.dtype)] + Gather.scratch(sizes["fsdp"])
        else:
            block = array.shape[1:]
            scratch += Reduce.scratch(n, block, array.dtype)
            if kind == "reduce":
                shapes.append(block)
            elif kind == "sum":
                shapes.append(array.shape)
                scratch += [pltpu.VMEM(block, dtype)] + Gather.scratch(n)
            else:
                shapes.append((sizes["fsdp"],) + block)
                scratch += [pltpu.VMEM(block, dtype)] + Gather.scratch(sizes["fsdp"])
    vmem = pl.BlockSpec(memory_space=pltpu.VMEM)
    return pl.pallas_call(
        functools.partial(comm_kernel, tuple((kind, axis) for kind, axis, _, _ in jobs)),
        out_shape=[jax.ShapeDtypeStruct(s, j[3]) for s, j in zip(shapes, jobs)],
        in_specs=[vmem] * len(jobs),
        out_specs=[vmem] * len(jobs),
        scratch_shapes=scratch,
        compiler_params=pltpu.CompilerParams(
            collective_id=number, has_side_effects=True, vmem_limit_bytes=60 * 1024 * 1024
        ),
    )(*[array for _, _, array, _ in jobs])


def with_halo(value, sides, width):
    for axis, dim in sides:
        devices, length = (lax.axis_size(axis), value.shape[dim])
        up = [(i, (i + 1) % devices) for i in range(devices - 1)]
        down = [(j, i) for i, j in up]
        last = lax.slice_in_dim(value, length - width, length, axis=dim)
        first = lax.slice_in_dim(value, 0, width, axis=dim)
        before = lax.ppermute(last, axis, up)
        after = lax.ppermute(first, axis, down)
        value = jnp.concatenate([before, value, after], axis=dim)
    return value


def norm_forward(values, gain):
    mean = jnp.mean(values, axis=-1, keepdims=True)
    centred = values - mean
    inverse = lax.rsqrt(jnp.mean(centred * centred, axis=-1, keepdims=True) + EPSILON)
    scaled = centred * inverse
    return (scaled, inverse, (scaled * gain.astype(jnp.float32)).astype(jnp.bfloat16))


def norm_backward(grad, scaled, inverse, gain):
    weighted = grad * gain.astype(jnp.float32)
    back = inverse * (
        weighted
        - jnp.mean(weighted, axis=-1, keepdims=True)
        - scaled * jnp.mean(weighted * scaled, axis=-1, keepdims=True)
    )
    return back


def gelu_parts(inner):
    cdf = 0.5 * (1.0 + jax.scipy.special.erf(inner * 0.7071067811865476))
    density = jnp.exp(-0.5 * inner * inner) * 0.3989422804014327
    return (inner * cdf, cdf + inner * density)


def rope_tables(positions, head_size):
    half = head_size // 2
    inv_freq = 10000.0 ** (-(2.0 / head_size) * jnp.arange(half, dtype=jnp.float32))
    angle = positions.astype(jnp.float32)[:, None] * inv_freq[None, :]
    return (jnp.cos(angle)[:, None, :], jnp.sin(angle)[:, None, :])


def rotate(field, cosine, sine):
    half = field.shape[-1] // 2
    first, second = (field[..., :half], field[..., half:])
    return jnp.concatenate(
        [first * cosine - second * sine, second * cosine + first * sine], axis=-1
    )


def unrotate(grad, cosine, sine):
    half = grad.shape[-1] // 2
    first, second = (grad[..., :half], grad[..., half:])
    return jnp.concatenate(
        [first * cosine + second * sine, second * cosine - first * sine], axis=-1
    )


def doc_ids(lengths_row, positions):
    starts = jnp.cumsum(lengths_row, dtype=jnp.int32) - lengths_row
    total = jnp.sum(lengths_row, dtype=jnp.int32)
    found = (
        jnp.sum((positions[:, None] >= starts[None, :]).astype(jnp.int32), axis=1, dtype=jnp.int32)
        - 1
    )
    valid = (positions >= 0) & (positions < total)
    return jnp.where(valid, found, -1)


def window_mask(ids_query, ids_key, reach):
    block = ids_query.shape[0]
    offset = (
        jnp.arange(block, dtype=jnp.int32)[:, None]
        + reach
        - jnp.arange(block + 2 * reach, dtype=jnp.int32)[None, :]
    )
    return (jnp.abs(offset) <= reach) & (ids_query[:, None] == ids_key[None, :])


def attend_forward(query, keys, values, allowed):
    scale = query.shape[-1] ** (-0.5)
    scores = jnp.einsum("nhe,mhe->hnm", query, keys, preferred_element_type=jnp.float32) * scale
    masked = jnp.where(allowed[None], scores, -1e30)
    top = jnp.max(masked, axis=-1, keepdims=True)
    expd = jnp.exp(masked - top)
    total = jnp.sum(expd, axis=-1, keepdims=True)
    log_total = (top + jnp.log(total))[..., 0]
    probs = (expd / total).astype(jnp.bfloat16)
    out = jnp.einsum("hnm,mhe->nhe", probs, values, preferred_element_type=jnp.float32)
    return (out.astype(jnp.bfloat16), log_total)


def attend_backward(query, keys, values, allowed, log_total, attended, grad_out):
    scale = query.shape[-1] ** (-0.5)
    scores = jnp.einsum("nhe,mhe->hnm", query, keys, preferred_element_type=jnp.float32) * scale
    masked = jnp.where(allowed[None], scores, -1e30)
    again = jnp.exp(masked - log_total[..., None])
    again_b = again.astype(jnp.bfloat16)
    grad_values = jnp.einsum("hnm,nhe->mhe", again_b, grad_out, preferred_element_type=jnp.float32)
    grad_probs = jnp.einsum("nhe,mhe->hnm", grad_out, values, preferred_element_type=jnp.float32)
    delta = jnp.sum(grad_out.astype(jnp.float32) * attended.astype(jnp.float32), axis=-1).T
    grad_scores = (again * (grad_probs - delta[..., None]) * scale).astype(jnp.bfloat16)
    grad_query = jnp.einsum("hnm,mhe->nhe", grad_scores, keys, preferred_element_type=jnp.float32)
    grad_keys = jnp.einsum("hnm,nhe->mhe", grad_scores, query, preferred_element_type=jnp.float32)
    return (grad_query, grad_keys, grad_values)


def attention_forward(query, ext_keys, ext_values, ids_query, ids_key, block, reach):
    rows, heads = (query.shape[0], query.shape[1])
    count = rows // block

    def step(carry, index):
        allowed = window_mask(ids_query, ids_key, reach)
        return (carry, attend_forward(query, ext_keys, ext_values, allowed))

    _, (outs, totals) = lax.scan(
        step, jnp.zeros((), jnp.float32), jnp.arange(count, dtype=jnp.int32)
    )
    return (outs.reshape(rows, heads, -1), totals.transpose(1, 0, 2).reshape(heads, rows))


def attention_backward(
    query, ext_keys, ext_values, ids_query, ids_key, log_total, attended, grad_out, block, reach
):
    rows = query.shape[0]
    count = rows // block
    zero = jnp.zeros(ext_keys.shape, jnp.float32)

    def step(carry, index):
        keys_acc, values_acc = carry
        allowed = window_mask(ids_query, ids_key, reach)
        grad_query, grad_keys, grad_values = attend_backward(
            query, ext_keys, ext_values, allowed, log_total, attended, grad_out
        )
        keys_acc = keys_acc + grad_keys
        values_acc = values_acc + grad_values
        return ((keys_acc, values_acc), grad_query)

    (keys_acc, values_acc), grads = lax.scan(step, (zero, zero), jnp.arange(count, dtype=jnp.int32))
    return (grads.reshape(query.shape), keys_acc, values_acc)


def per_device(
    layer_input,
    doc_lengths,
    attn_gain,
    qkv_weight,
    out_weight,
    mlp_gain,
    in_weight,
    down_weight,
    out_grad,
):
    tokens = layer_input[0]
    grad_rows = out_grad[0]
    rows, width = tokens.shape
    streams = doc_lengths.shape[0]
    quarter = qkv_weight.shape[2]
    heads_here = quarter // HEAD
    share = down_weight.shape[1]
    reach = WIN
    block = min(rows, 512)
    n_seq, n_fsdp = lax.axis_size("seq"), lax.axis_size("fsdp")
    stream = lax.axis_index("fsdp")
    part = width // n_seq
    piece = attn_gain.shape[0]
    b16, f32 = jnp.bfloat16, jnp.float32
    first = lax.axis_index("seq") * rows
    positions = first + jnp.arange(rows, dtype=jnp.int32)
    outer = first - reach + jnp.arange(rows + 2 * reach, dtype=jnp.int32)
    ids_query = jax.vmap(doc_ids, in_axes=(0, None))(doc_lengths, positions)
    ids_key = jax.vmap(doc_ids, in_axes=(0, None))(doc_lengths, outer)
    cosine, sine = rope_tables(positions, HEAD)
    gains = jnp.pad(jnp.stack([attn_gain, mlp_gain]), ((0, 14), (0, 128 - piece)))
    gains_all, rim_all, tokens_all, qkv_all, out_all = communicate(
        1,
        [
            ("gather2", "seq", gains, b16),
            ("halo", "both", tokens, b16),
            ("gather", "fsdp", tokens, b16),
            ("gather", "seq", qkv_weight.reshape(part, 3 * quarter), b16),
            ("gather", "seq", out_weight, b16),
        ],
    )
    gain_one = gains_all[:, :, 0, :piece].transpose(1, 0, 2).reshape(width)
    gain_two = gains_all[:, :, 1, :piece].transpose(1, 0, 2).reshape(width)
    qkv_flat = qkv_all.reshape(width, 3 * quarter)
    out_rows = out_all.transpose(1, 0, 2).reshape(quarter, width)
    resid_in = tokens_all.reshape(streams * rows, width).astype(f32)
    scaled_one, inverse_one, group_one = norm_forward(resid_in, gain_one)
    rim_rows = streams * 2 * reach
    normed_rim = norm_forward(rim_all.reshape(rim_rows, width).astype(f32), gain_one)[2]
    normed_rim = normed_rim.reshape(streams, 2, reach, width)
    normed_outer = jnp.concatenate(
        [normed_rim[:, 0], group_one.reshape(streams, rows, width), normed_rim[:, 1]], axis=1
    ).reshape(streams * (rows + 2 * reach), width)
    outer_cosine, outer_sine = rope_tables(outer, HEAD)
    projected = jnp.dot(group_one, qkv_flat[:, :quarter], preferred_element_type=f32)
    query = rotate(projected.reshape(streams, rows, heads_here, HEAD), cosine, sine).astype(b16)
    projected = jnp.dot(normed_outer, qkv_flat[:, quarter:], preferred_element_type=f32)
    split = projected.reshape(streams, rows + 2 * reach, 2, heads_here, HEAD)
    ext_keys = rotate(split[:, :, 0], outer_cosine, outer_sine).astype(b16)
    ext_values = split[:, :, 1].astype(b16)

    def forward_stream(stream_query, stream_keys, stream_values, stream_ids, stream_key_ids):
        return attention_forward(
            stream_query, stream_keys, stream_values, stream_ids, stream_key_ids, block, reach
        )

    attended, log_total = jax.vmap(forward_stream)(query, ext_keys, ext_values, ids_query, ids_key)
    attended_flat = attended.reshape(streams * rows, quarter)
    partial_attn = jnp.dot(attended_flat, out_rows, preferred_element_type=f32)
    attn_sum, grad_all, in_all, down_all = communicate(
        2,
        [
            ("sum", "fsdp", partial_attn.astype(b16).reshape(streams, rows, width), b16),
            ("gather", "fsdp", grad_rows, b16),
            ("gather", "seq", in_weight.reshape(part, 2 * share), b16),
            ("gather", "seq", down_weight, b16),
        ],
    )
    in_flat = in_all.reshape(width, 2 * share)
    down_full = down_all.reshape(width, share)
    grad_flat = grad_all.reshape(streams * rows, width)
    middle = resid_in + attn_sum.reshape(streams * rows, width).astype(f32)
    scaled_two, inverse_two, normed_flat = norm_forward(middle, gain_two)
    hidden = jnp.dot(normed_flat, in_flat, preferred_element_type=f32)
    inner, gate = (hidden[:, :share], hidden[:, share:])
    activated, slope = gelu_parts(inner)
    mixed = (activated * gate).astype(b16)
    partial_down = lax.dot_general(
        mixed, down_full, (((1,), (1,)), ((), ())), preferred_element_type=f32
    )
    grad_down = lax.dot_general(
        grad_flat, mixed, (((0,), (0,)), ((), ())), preferred_element_type=f32
    )
    grad_mixed = jnp.dot(grad_flat, down_full, preferred_element_type=f32)
    grad_hidden = jnp.concatenate(
        [grad_mixed * gate * slope, grad_mixed * activated], axis=1
    ).astype(b16)
    grad_in = lax.dot_general(
        normed_flat, grad_hidden, (((0,), (0,)), ((), ())), preferred_element_type=f32
    )
    partial_back = lax.dot_general(
        grad_hidden, in_flat, (((1,), (1,)), ((), ())), preferred_element_type=f32
    )
    grad_gain_two = jnp.sum(partial_back * scaled_two, axis=0)
    back_sum, down_sum, summed_in, summed_down = communicate(
        3,
        [
            ("sum", "fsdp", partial_back.astype(b16).reshape(streams, rows, width), b16),
            ("reduce", "fsdp", partial_down.astype(b16).reshape(streams, rows, width), f32),
            ("reduce", "seq", grad_in.astype(b16).reshape(n_seq, part, 2 * share), f32),
            ("reduce", "seq", grad_down.astype(b16).reshape(n_seq, part, share), f32),
        ],
    )
    middle_own = lax.dynamic_slice_in_dim(middle, stream * rows, rows, axis=0)
    output = (middle_own + down_sum).astype(b16)
    back_two = norm_backward(
        back_sum.reshape(streams * rows, width).astype(f32), scaled_two, inverse_two, gain_two
    )
    grad_middle = grad_flat.astype(f32) + back_two
    grad_group = grad_middle.astype(b16)
    grad_out_weight = lax.dot_general(
        grad_group, attended_flat, (((0,), (0,)), ((), ())), preferred_element_type=f32
    )
    grad_attended = lax.dot_general(
        grad_group, out_rows, (((1,), (1,)), ((), ())), preferred_element_type=f32
    ).astype(b16)

    def backward_stream(
        stream_query,
        stream_keys,
        stream_values,
        stream_ids,
        stream_key_ids,
        stream_total,
        stream_attended,
        stream_grad,
    ):
        return attention_backward(
            stream_query,
            stream_keys,
            stream_values,
            stream_ids,
            stream_key_ids,
            stream_total,
            stream_attended,
            stream_grad,
            block,
            reach,
        )

    grad_query, keys_acc, values_acc = jax.vmap(backward_stream)(
        query,
        ext_keys,
        ext_values,
        ids_query,
        ids_key,
        log_total,
        attended,
        grad_attended.reshape(streams, rows, heads_here, HEAD),
    )
    rims = jnp.concatenate(
        [keys_acc.reshape(streams, -1, quarter), values_acc.reshape(streams, -1, quarter)], axis=2
    )
    edges = jnp.concatenate([rims[:, :reach], rims[:, -reach:]], axis=1)
    arrived = with_halo(edges.astype(jnp.bfloat16), (("seq", 1),), WIN).astype(edges.dtype)
    owned = (
        rims[:, reach : reach + rows]
        + jnp.pad(arrived[:, :reach], ((0, 0), (0, rows - reach), (0, 0)))
        + jnp.pad(arrived[:, -reach:], ((0, 0), (rows - reach, 0), (0, 0)))
    )
    grad_keys = unrotate(
        owned[:, :, :quarter].reshape(streams, rows, heads_here, HEAD), cosine, sine
    )
    grad_values = owned[:, :, quarter:]
    grad_query = unrotate(grad_query, cosine, sine)
    grad_projected = jnp.concatenate(
        [
            grad_query.reshape(streams * rows, quarter),
            grad_keys.reshape(streams * rows, quarter),
            grad_values.reshape(streams * rows, quarter),
        ],
        axis=1,
    ).astype(jnp.bfloat16)
    grad_qkv = lax.dot_general(
        group_one, grad_projected, (((0,), (0,)), ((), ())), preferred_element_type=f32
    )
    partial_one = lax.dot_general(
        grad_projected, qkv_flat, (((1,), (1,)), ((), ())), preferred_element_type=f32
    )
    grad_gain_one = jnp.sum(partial_one * scaled_one, axis=0)
    gain_parts = jnp.stack([grad_gain_one, grad_gain_two]).reshape(2, n_seq, part)
    gain_parts = jnp.pad(gain_parts.transpose(1, 0, 2), ((0, 0), (0, 6), (0, -part % 128)))
    gain_sums, one_sum, summed_qkv, summed_out = communicate(
        4,
        [
            ("reduce2", "seq", gain_parts, f32),
            ("reduce", "fsdp", partial_one.astype(b16).reshape(streams, rows, width), f32),
            ("reduce", "seq", grad_qkv.astype(b16).reshape(n_seq, part, 3 * quarter), f32),
            ("reduce", "seq", grad_out_weight.astype(b16).reshape(n_seq, part, quarter), f32),
        ],
    )
    gain_sum = lax.dynamic_slice_in_dim(jnp.sum(gain_sums, axis=0), stream * piece, piece, axis=1)

    def own_rows(array):
        return lax.dynamic_slice_in_dim(array, stream * rows, rows, axis=0)

    back_one = norm_backward(one_sum, own_rows(scaled_one), own_rows(inverse_one), gain_one)
    input_grad = own_rows(grad_middle) + back_one
    return (
        output[None],
        input_grad[None],
        gain_sum[0],
        summed_qkv.reshape(part, 3, quarter),
        summed_out.T,
        gain_sum[1],
        summed_in.reshape(part, 2, share),
        summed_down,
    )


def solution(mesh):
    in_specs = (
        P("fsdp", "seq", None),
        P(),
        P(("seq", "fsdp")),
        P("seq", None, "fsdp"),
        P("fsdp", "seq"),
        P(("seq", "fsdp")),
        P("seq", None, "fsdp"),
        P("seq", "fsdp"),
        P("fsdp", "seq", None),
    )
    out_specs = (
        P("fsdp", "seq", None),
        P("fsdp", "seq", None),
        P(("seq", "fsdp")),
        P("seq", None, "fsdp"),
        P("fsdp", "seq"),
        P(("seq", "fsdp")),
        P("seq", None, "fsdp"),
        P("seq", "fsdp"),
    )
    return jax.shard_map(
        per_device, mesh=mesh, in_specs=in_specs, out_specs=out_specs, check_vma=False
    )
```
